32 devices in a mesh: groups: 2 (over y), ctx: 4 (over z), dp: 4 (over x, core).
Axes of the slice: x: 2, y: 2, z: 4, core: 2. Of those that a mesh axis runs over, the one named last changes fastest.
Arguments:
- hidden: bfloat16 [8, 2048, 768], P(('groups', 'dp'), 'ctx'), parts along dimension 0, may hold values from -24 to 24
- w_qkv: bfloat16 [768, 1152], replicated, may hold values from -0.21875 to 0.21875
- doc_lengths: int32 [8, 8], P(('groups', 'dp')), parts along dimension 0, may hold values from 1 to 1024, 2048 in all within a row
- grad_context: bfloat16 [8, 2048, 384], P(('groups', 'dp'), 'ctx'), parts along dimension 0, may hold values from -6 to 6
Outputs:
- context: bfloat16 [8, 2048, 384], P(('groups', 'dp'), 'ctx'), parts along dimension 0
- grad_hidden: bfloat16 [8, 2048, 768], P(('groups', 'dp'), 'ctx'), parts along dimension 0
- grad_weight: float32 [1536, 1152], P(('groups', 'ctx', 'dp')), parts along dimension 0
The draws below stay inside these ranges and needn't reach their ends.
There are 2 independent parts, one for each index of `groups`. The reference program is written for one: setup_inputs(seed, part) draws one part's arguments, and reference() takes and returns one part's arrays. A program takes and returns all parts, laid end to end along the dimension named above; an argument that names none is the same for every part. Nothing has to cross between parts.
Inputs may be any that keep to these rules, and one draw needn't show every extreme that they name: `doc_lengths`: each row holds the lengths of the 8 documents of one sequence; they sum to 2048.
All inputs are finite; a program needn't handle non-finite values.
Results may differ from the reference program's by a relative error of at most 0.018.
The reference program's roundings to bfloat16 on the way (of `chance_low`, `grad_score` and `grad_proj`) count: a program that leaves them out, or rounds other values in their place, can miss the bound.
Values may be sent and summed in bfloat16 or wider, within the bound.
A program may use at most 64 MiB of HBM per device.

```python
import math
import jax
import jax.numpy as jnp
import numpy as np
from jax import lax

D = 768
HEADS = 6
HEAD_DIM = 64
HALF = 64
TOK_DEV = 512
INNER = 384
POSITION_COUNT = 2048
STREAM_COUNT = 4
DOCS = 8


def draw_hidden(key, part):
    noise_key = jax.random.fold_in(key, 11)
    pairing_key = jax.random.fold_in(key, 12)
    slab_count = POSITION_COUNT // TOK_DEV
    block_count = slab_count * STREAM_COUNT
    block_width = D // block_count
    pairing = jax.random.permutation(pairing_key, block_count)
    feature_block = jnp.arange(D) // block_width
    slab_tag = jnp.arange(STREAM_COUNT)[:, None] * slab_count + jnp.arange(POSITION_COUNT)[None, :] // TOK_DEV
    chosen = pairing[slab_tag]
    boosted = jnp.where(chosen[:, :, None] == feature_block[None, None, :], 4.0, 1.0).astype(jnp.float32)
    base_draw = jnp.clip(jax.random.normal(noise_key, (STREAM_COUNT, POSITION_COUNT, D), jnp.float32), -6.0, 6.0)
    return (base_draw * boosted).astype(jnp.bfloat16)


def block_scale(own_key, shape, cuts, smallest, high):
    factor_of, own = 1.0, jax.random.fold_in(own_key, 6)
    for axis_at, parts in cuts:
        steps = jnp.exp(jax.random.uniform(jax.random.fold_in(own, axis_at), (parts,), jnp.float32, smallest / len(cuts), high / len(cuts)))
        factor_of = factor_of * jnp.repeat(steps, shape[axis_at] // parts).reshape([-1 if axis == axis_at else 1 for axis in range(len(shape))])
    return factor_of


def split_up(count, total, reach, lean):
    weights = [(1 << 20) // math.isqrt(grade ** lean) + 1 for grade in range(2, count + 1)]
    spare, holding = total - reach - (count - 1), [1] * (count - 1)
    while spare > 0:
        movable = [i for i in range(count - 1) if holding[i] < reach]
        whole, budget = sum([weights[i] for i in movable]), spare
        for i in movable:
            extra = min(reach - holding[i], max(1, budget * weights[i] // whole), spare)
            holding[i] = holding[i] + extra
            spare = spare - extra
    return np.array([reach] + holding)


def uneven(rng, amount, total, bound, skew):
    if amount == 2:
        one = jax.random.randint(rng, (), max(1, total - bound), min(bound, total - 1) + 1)
        return jnp.stack([one, total - one])
    tallies = jnp.asarray(split_up(amount, total, bound, skew), jnp.int32)
    twos = (amount - 1) // 2
    source_of, sink = tallies[1:1 + 2 * twos:2], tallies[2:2 + 2 * twos:2]
    room = jnp.minimum(source_of - 1, bound - sink)
    shifted = jax.random.randint(jax.random.fold_in(rng, 1), (twos,), 0, 1 << 20) % (room + 1)
    tallies = tallies.at[1:1 + 2 * twos:2].set(source_of - shifted).at[2:2 + 2 * twos:2].set(sink + shifted)
    return tallies[jax.random.permutation(jax.random.fold_in(rng, 2), amount)]


def scatter_about(key, shape, deviation, bound, shards=(), kind=jnp.bfloat16):
    result = jax.random.normal(key, shape, jnp.float32) * deviation
    if len(shards) > 0:
        result = block_scale(key, shape, shards, -0.22, 0.18) * result
    return jnp.clip(result, min=-bound, max=bound).astype(kind)


def setup_inputs(seed: int = 0, part: int = 0) -> dict:
    seeds = jax.random.split(jax.random.key(seed), 5)
    part_keys = jax.random.split(jax.random.fold_in(seeds[4], part), 5)
    hidden = draw_hidden(jax.random.fold_in(jax.random.fold_in(seeds[4], part), 71), part)
    w_qkv = scatter_about(seeds[1], (D, 3 * INNER), D ** -0.5, 0.21875)
    doc_lengths = jax.vmap(lambda own: uneven(own, DOCS, POSITION_COUNT, 2 * TOK_DEV, 1))(jax.random.split(part_keys[2], STREAM_COUNT)).reshape((STREAM_COUNT, DOCS)).astype(jnp.int32)
    grad_context = scatter_about(part_keys[3], (STREAM_COUNT, POSITION_COUNT, INNER), 1.0, 6.0, ((0, 4), (1, 4)))
    return {"hidden": hidden, "w_qkv": w_qkv, "doc_lengths": doc_lengths, "grad_context": grad_context}


masked_value = -1e30
block_cap = 512


def rotate(matrix, positions, sign_factor):
    half_dim = HEAD_DIM // 2
    row_count = matrix.shape[0]
    frequency = 10000.0 ** (-(jnp.arange(half_dim, dtype=jnp.float32) * 2.0 / HEAD_DIM))
    angles = positions.astype(jnp.float32)[:, None] * frequency[None, :]
    cosine = jnp.cos(angles)[:, None, :]
    sine_part = sign_factor * jnp.sin(angles)[:, None, :]
    shaped = matrix.reshape(row_count, -1, HEAD_DIM)
    front_half = shaped[:, :, :half_dim]
    back_half = shaped[:, :, half_dim:]
    turned = jnp.concatenate([front_half * cosine - back_half * sine_part, back_half * cosine + front_half * sine_part], axis=2)
    return turned.reshape(row_count, -1)


def doc_ids(document_end_index, positions):
    return jnp.sum((document_end_index[None, :] <= positions[:, None]).astype(jnp.int32), axis=1, dtype=jnp.int32)


def to_low(matrix):
    return lax.optimization_barrier(matrix.astype(jnp.bfloat16)).astype(jnp.float32)


def split_heads(matrix):
    return matrix.astype(jnp.float32).reshape(matrix.shape[0], HEADS, HEAD_DIM)


def attend_all(queries, keys_in, values_in, grads_out, allowed):
    q_count = queries.shape[0]
    k_count = keys_in.shape[0]
    scale = HEAD_DIM ** -0.5
    query_full = split_heads(queries)
    key_full = split_heads(keys_in)
    value_full = split_heads(values_in)
    grad_full = split_heads(grads_out)
    scores = jnp.einsum("qhd,khd->hqk", query_full, key_full) * scale
    scores = jnp.where(allowed[None], scores, masked_value)
    row_max = jnp.max(scores, axis=2, keepdims=True)
    log_total = row_max + jnp.log(jnp.sum(jnp.exp(scores - row_max), axis=2, keepdims=True))
    likelihood = jnp.exp(scores - log_total)
    chance_low = to_low(likelihood)
    context = jnp.einsum("hqk,khd->qhd", chance_low, value_full).reshape(q_count, -1).astype(jnp.bfloat16)
    row_delta = jnp.sum(grad_full * split_heads(context), axis=2).T
    grad_chance = jnp.einsum("qhd,khd->hqk", grad_full, value_full)
    grad_score = to_low(likelihood * (grad_chance - row_delta[:, :, None]))
    grad_query = jnp.einsum("hqk,khd->qhd", grad_score, key_full).reshape(q_count, -1) * scale
    grad_key = jnp.einsum("hqk,qhd->khd", grad_score, query_full).reshape(k_count, -1) * scale
    grad_value = jnp.einsum("hqk,qhd->khd", chance_low, grad_full).reshape(k_count, -1)
    return context, grad_query, grad_key, grad_value


def join_blocks(extended, q_block):
    middle = extended[:, HALF:HALF + q_block]
    middle = middle.at[:-1, q_block - HALF:].add(extended[1:, :HALF])
    middle = middle.at[1:, :HALF].add(extended[:-1, q_block + HALF:])
    return middle.reshape(-1, middle.shape[2])


def sequence_pass(tokens, doc_lengths, upstream, w_qkv):
    seq_len = tokens.shape[0]
    inner_width = HEADS * HEAD_DIM
    q_block = min(TOK_DEV, block_cap)
    k_reach = q_block + 2 * HALF
    block_count = seq_len // q_block
    positions = jnp.arange(seq_len, dtype=jnp.int32)
    document_end_index = jnp.cumsum(doc_lengths, dtype=jnp.int32)
    q_doc = doc_ids(document_end_index, positions)
    k_pos = jnp.arange(seq_len + 2 * HALF, dtype=jnp.int32) - HALF
    k_doc = doc_ids(document_end_index, k_pos)
    k_live = (k_pos >= 0) & (k_pos < seq_len)
    projected = jnp.dot(tokens, w_qkv, preferred_element_type=jnp.float32)
    queries = rotate(projected[:, :inner_width], positions, 1.0).astype(jnp.bfloat16)
    keys_own = rotate(projected[:, inner_width:2 * inner_width], positions, 1.0).astype(jnp.bfloat16)
    values = projected[:, 2 * inner_width:].astype(jnp.bfloat16)
    keys_pad = jnp.pad(keys_own, ((HALF, HALF), (0, 0)))
    values_pad = jnp.pad(values, ((HALF, HALF), (0, 0)))

    def one_block(block_index):
        first_row = (block_index * q_block).astype(jnp.int32)
        q_near = lax.dynamic_slice_in_dim(positions, first_row, q_block, 0)
        k_near = lax.dynamic_slice_in_dim(k_pos, first_row, k_reach, 0)
        q_docs = lax.dynamic_slice_in_dim(q_doc, first_row, q_block, 0)
        k_docs = lax.dynamic_slice_in_dim(k_doc, first_row, k_reach, 0)
        k_alive = lax.dynamic_slice_in_dim(k_live, first_row, k_reach, 0)
        allowed = (jnp.abs(q_near[:, None] - k_near[None, :]) <= HALF) & (q_docs[:, None] == k_docs[None, :]) & k_alive[None, :]
        return attend_all(
            lax.dynamic_slice_in_dim(queries, first_row, q_block, 0),
            lax.dynamic_slice_in_dim(keys_pad, first_row, k_reach, 0),
            lax.dynamic_slice_in_dim(values_pad, first_row, k_reach, 0),
            lax.dynamic_slice_in_dim(upstream, first_row, q_block, 0),
            allowed)

    context, grad_query, grad_key, grad_value = lax.map(one_block, jnp.arange(block_count, dtype=jnp.int32))
    context = context.reshape(seq_len, inner_width)
    grad_query = grad_query.reshape(seq_len, inner_width)
    grad_key = join_blocks(grad_key, q_block)
    grad_value = join_blocks(grad_value, q_block)
    grad_proj = jnp.concatenate([rotate(grad_query, positions, -1.0), rotate(grad_key, positions, -1.0), grad_value], axis=1).astype(jnp.bfloat16)
    grad_hidden = lax.dot_general(grad_proj, w_qkv, (((1,), (1,)), ((), ())), preferred_element_type=jnp.float32).astype(jnp.bfloat16)
    grad_weight = lax.dot_general(tokens, grad_proj, (((0,), (0,)), ((), ())), preferred_element_type=jnp.float32)
    return context, grad_hidden, grad_weight


def reference(hidden, w_qkv, doc_lengths, grad_context):
    def one_sequence(inputs):
        return sequence_pass(inputs[0], inputs[1], inputs[2], w_qkv)

    context, grad_hidden, grad_weight = lax.map(one_sequence, (hidden, doc_lengths, grad_context))
    return context, grad_hidden, jnp.sum(grad_weight, axis=0)
```

```python
import functools

import jax
import jax.numpy as jnp
import numpy as np
from jax import lax
from jax.experimental import pallas as pl
from jax.experimental.pallas import tpu as pltpu
from jax.sharding import PartitionSpec as P

HEAD_DIM = 64
HALF = 64
LANES = 128
REACH = 2 * HALF
masked_value = -1e30
MESH = pl.DeviceIdType.MESH


def angle_tables(rows, slabs, tok_rows):
    half_dim = HEAD_DIM // 2
    exponent = np.arange(half_dim, dtype=np.float64) * 2.0 / HEAD_DIM
    frequency = 10000.0 ** (-exponent)

    def table(positions):
        angles = positions[:, None] * frequency[None, :]
        cosine = np.tile(np.cos(angles), (1, LANES // half_dim))
        sine = np.sin(angles)
        signed = np.tile(np.concatenate([-sine, sine], axis=1), (1, LANES // HEAD_DIM))
        return np.concatenate([cosine, signed], axis=1).astype(np.float32)

    near = table(np.arange(rows, dtype=np.float64) - REACH)
    base = table(np.arange(slabs, dtype=np.float64) * tok_rows)
    return near, np.repeat(base, 8, axis=0)


def kernel(
    slabs, spread, doc_lengths, base, hidden_hbm, w_hbm, grads_hbm, near_hbm,
    context, grad_hidden, grad_weight,
    hidden, w, grads, near, before, after, grads_before, grads_after,
    queries, keys, values, keys_t, values_t, upstream, tables, biases, key_acc, value_acc,
    grad_proj, hidden_t, load_sem, rim_send, rim_recv, *summing,
):
    tok_rows, width = hidden.shape
    inner = grads.shape[1]
    pairs = inner // LANES
    rows = tok_rows + 2 * REACH
    tiles = tok_rows // LANES + 1
    doc_count = doc_lengths.shape[1]
    slab = lax.axis_index("ctx")
    offset = slab * tok_rows

    loads = [
        pltpu.make_async_copy(source, target, load_sem.at[i])
        for i, (source, target) in enumerate(
            ((hidden_hbm, hidden), (grads_hbm, grads), (w_hbm, w), (near_hbm, near))
        )
    ]
    for load in loads:
        load.start()

    replica = lax.axis_index("dp")
    core, chip = lax.rem(replica, 2), lax.div(replica, 2)
    core_peer = {"dp": replica + 1 - 2 * core}
    chip_peer = {"dp": replica + 2 - 4 * chip}
    slab_peers = [lax.rem(slab + k, slabs) for k in range(1, slabs)]
    barrier = pltpu.get_barrier_semaphore()
    has_before, has_after = slab > 0, slab < slabs - 1

    def greet(peer):
        pl.semaphore_signal(barrier, inc=1, device_id=peer, device_id_type=MESH)

    if spread:
        for peer in [core_peer, chip_peer] + [{"ctx": other} for other in slab_peers]:
            greet(peer)
    else:
        pl.when(has_before)(lambda: greet({"ctx": slab - 1}))
        pl.when(has_after)(lambda: greet({"ctx": slab + 1}))

    def wait_for_all():
        if spread:
            pl.semaphore_wait(barrier, slabs + 1)
        else:
            pl.when(has_before)(lambda: pl.semaphore_wait(barrier, 1))
            pl.when(has_after)(lambda: pl.semaphore_wait(barrier, 1))

    def remote(source, target, send, recv, peer):
        return pltpu.make_async_remote_copy(
            src_ref=source, dst_ref=target, send_sem=send, recv_sem=recv,
            device_id=peer, device_id_type=MESH,
        )

    def rim(source, start, target, index, to):
        return remote(
            source.at[pl.ds(start, target.shape[0])], target,
            rim_send.at[index], rim_recv.at[index], {"ctx": to},
        )

    rims_up = [
        rim(hidden, tok_rows - REACH, before, 0, slab + 1),
        rim(grads, tok_rows - HALF, grads_before, 1, slab + 1),
    ]
    rims_down = [
        rim(hidden, 0, after, 2, slab - 1),
        rim(grads, 0, grads_after, 3, slab - 1),
    ]

    def every(copies, act):
        for copy in copies:
            getattr(copy, act)()

    lane = lax.broadcasted_iota(jnp.int32, (1, LANES), 1)
    front = lax.rem(lane, HEAD_DIM) < HEAD_DIM // 2
    first = (lane < HEAD_DIM).astype(jnp.bfloat16)
    second = (lane >= HEAD_DIM).astype(jnp.bfloat16)

    def swapped(block):
        half = HEAD_DIM // 2
        return jnp.where(
            front, pltpu.roll(block, LANES - half, 1), pltpu.roll(block, half, 1)
        )

    def rotate(block, start, sign):
        size = block.shape[0]
        turned = block * tables[pl.ds(start, size), :LANES]
        other = swapped(block) * tables[pl.ds(start, size), LANES:]
        return turned + other if sign > 0 else turned - other

    ends = []
    total = jnp.int32(0)
    for j in range(doc_count):
        total = total + doc_lengths[0, j]
        ends.append(total)

    def doc_of(positions):
        found = (positions >= 0).astype(jnp.int32)
        for end in ends:
            found = found + (end <= positions).astype(jnp.int32)
        return found

    key_at = lax.broadcasted_iota(jnp.int32, (2 * LANES, LANES), 0)
    query_at = lax.broadcasted_iota(jnp.int32, (2 * LANES, LANES), 1) + HALF
    in_band = jnp.abs(query_at - key_at) <= HALF
    k_col = lax.broadcasted_iota(jnp.int32, (2 * LANES, 1), 0)
    q_row = lax.broadcasted_iota(jnp.int32, (1, LANES), 1)
    for tile in range(tiles):
        k_first = offset - REACH + tile * LANES
        k_doc = doc_of(k_col + k_first)
        q_doc = doc_of(q_row + (k_first + HALF))
        allowed = in_band & (k_doc == q_doc)
        biases[tile] = jnp.where(allowed, 0.0, masked_value).astype(jnp.float32)

    wait_for_all()
    loads[0].wait()
    loads[1].wait()
    pl.when(has_after)(lambda: every(rims_up, "start"))
    pl.when(has_before)(lambda: every(rims_down, "start"))
    loads[3].wait()
    own_base = base[pl.ds(pl.multiple_of(slab * 8, 8), 8), :]
    base_cos = own_base[:1, :LANES]
    base_sin = own_base[:1, LANES:]
    near_cos = near[:, :LANES]
    near_sin = near[:, LANES:]
    tables[:, :LANES] = near_cos * base_cos - near_sin * base_sin
    tables[:, LANES:] = near_sin * base_cos + near_cos * base_sin

    def project(source, source_start, start, size):
        block = source[pl.ds(source_start, size), :]
        for part in range(3):
            columns = jnp.dot(
                block,
                w[:, part * inner : (part + 1) * inner],
                preferred_element_type=jnp.float32,
            )
            for pair in range(pairs):
                piece = columns[:, pair * LANES : (pair + 1) * LANES]
                if part == 0:
                    turned = rotate(piece, start, 1)
                    queries[pair, pl.ds(start, size), :] = turned.astype(
                        jnp.bfloat16
                    ) * jnp.bfloat16(HEAD_DIM**-0.5)
                else:
                    keep, keep_t = (keys, keys_t) if part == 1 else (values, values_t)
                    turned = rotate(piece, start, 1) if part == 1 else piece
                    keep[pair, pl.ds(start, size), :] = turned.astype(jnp.bfloat16)
                    keep_t[pair, :, pl.ds(start, size)] = turned.T.astype(jnp.bfloat16)

    def take_grads(source, source_start, start, size):
        for pair in range(pairs):
            upstream[pair, pl.ds(start, size), :] = source[
                pl.ds(source_start, size), pair * LANES : (pair + 1) * LANES
            ]

    step_rows = 2 * LANES
    loads[2].wait()
    for start in range(0, tok_rows, step_rows):
        project(hidden, start, REACH + start, step_rows)
        take_grads(grads, start, REACH + start, step_rows)
    turned_hidden = hidden[...].T
    if spread:
        share = width // (4 * slabs)
        for index in range(4 * slabs):
            at = (index % 4 // 2 * slabs + index // 4) * share
            hidden_t[index % 2, at : at + share, :] = turned_hidden[
                index * share : (index + 1) * share
            ]
    else:
        hidden_t[0] = turned_hidden

    def attend(pair, tile):
        q0, k0 = HALF + tile * LANES, tile * LANES
        key = keys[pair, pl.ds(k0, 2 * LANES), :]
        value = values[pair, pl.ds(k0, 2 * LANES), :]
        query = queries[pair, pl.ds(q0, LANES), :]
        grad = upstream[pair, pl.ds(q0, LANES), :]
        two_queries = jnp.concatenate([query * first, query * second], axis=0)
        two_grads = jnp.concatenate([grad * first, grad * second], axis=0)
        last = (((1,), (1,)), ((), ()))
        scores = lax.dot_general(key, two_queries, last, preferred_element_type=jnp.float32)
        bias = biases[tile]
        scores = scores + jnp.concatenate([bias, bias], axis=1)
        top = jnp.max(scores, axis=0, keepdims=True)
        raised = jnp.exp(scores - top)
        chance = raised * (1.0 / jnp.sum(raised, axis=0, keepdims=True))
        chance_low = chance.astype(jnp.bfloat16)

        def own_heads(both):
            return jnp.concatenate([both[:HEAD_DIM, :LANES], both[HEAD_DIM:, LANES:]], axis=0)

        mixture = own_heads(
            jnp.dot(
                values_t[pair, :, pl.ds(k0, 2 * LANES)],
                chance_low,
                preferred_element_type=jnp.float32,
            )
        )
        mixed = mixture.astype(jnp.bfloat16).astype(jnp.float32)
        product = grad.astype(jnp.float32).T * mixed
        delta = jnp.concatenate(
            [
                jnp.sum(product[:HEAD_DIM], axis=0, keepdims=True),
                jnp.sum(product[HEAD_DIM:], axis=0, keepdims=True),
            ],
            axis=1,
        )
        grad_chance = lax.dot_general(value, two_grads, last, preferred_element_type=jnp.float32)
        grad_score = (chance * (grad_chance - delta)).astype(jnp.bfloat16)
        query_grad = own_heads(
            jnp.dot(
                keys_t[pair, :, pl.ds(k0, 2 * LANES)],
                grad_score,
                preferred_element_type=jnp.float32,
            )
        ).T * (HEAD_DIM**-0.5)
        query_grad = rotate(query_grad, q0, -1).astype(jnp.bfloat16)
        mixed = mixed.T.astype(jnp.bfloat16)
        low = HALF if tile == 0 else 0
        high = HALF if tile == tiles - 1 else LANES
        out = q0 - REACH + low
        columns = pl.ds(pl.multiple_of(pair * LANES, LANES), LANES)
        context[pl.ds(out, high - low), columns] = mixed[low:high]
        grad_proj[pl.ds(out, high - low), columns] = query_grad[low:high]
        key_grad = jnp.dot(grad_score, two_queries, preferred_element_type=jnp.float32)
        value_grad = jnp.dot(chance_low, two_grads, preferred_element_type=jnp.float32)
        return key_grad, value_grad

    def add_to(pair, tile, pieces, seen):
        for acc, piece in zip((key_acc, value_acc), pieces):
            for part in range(2):
                block = tile + part - 1
                if 0 <= block < tiles - 1:
                    at = pl.ds(block * LANES, LANES)
                    part_rows = piece[part * LANES : (part + 1) * LANES]
                    if block in seen:
                        acc[at, :] += part_rows
                    else:
                        acc[at, :] = part_rows
        seen.update((tile - 1, tile))

    if spread:
        (
            kept, sent_1, got_1, kept_2, sent_2, got_2, kept_3, sent_3, got_3,
            send_1, recv_1, send_2, recv_2, send_3, recv_3,
        ) = summing

        def copy_1(pair):
            return remote(
                sent_1.at[pair], got_1.at[pair], send_1.at[pair], recv_1.at[pair], core_peer
            )

        def copy_2(pair):
            return remote(
                sent_2.at[pair], got_2.at[pair], send_2.at[pair], recv_2.at[pair], chip_peer
            )

        def copies_3(pair):
            return [
                remote(
                    sent_3.at[pair, other], got_3.at[pair, k],
                    send_3.at[pair, k], recv_3.at[pair, k], {"ctx": other},
                )
                for k, other in enumerate(slab_peers)
            ]

    def first_step(pair):
        for half, mine in ((1 - core, False), (core, True)):
            rows_in = hidden_t[half]
            for part in range(3):
                columns = pl.ds(pl.multiple_of(part * inner + pair * LANES, LANES), LANES)
                piece = jnp.dot(
                    rows_in, grad_proj[:, columns], preferred_element_type=jnp.float32
                ).reshape(2, -1, LANES)
                at = slice(part * LANES, (part + 1) * LANES)
                if mine:
                    kept[:, :, at] = piece
                else:
                    sent_1[pair, :, :, at] = piece.astype(jnp.bfloat16)
            if not mine:
                copy_1(pair).start()

    def middle_step(pair):
        copy_1(pair).wait_recv()
        away = 1 - chip
        sent_2[pair] = (kept[away] + got_1[pair, away].astype(jnp.float32)).astype(jnp.bfloat16)
        copy_2(pair).start()
        kept_2[pair] = kept[chip] + got_1[pair, chip].astype(jnp.float32)

    def second_step(pair):
        copy_2(pair).wait_recv()
        both = (kept_2[pair] + got_2[pair].astype(jnp.float32)).reshape(slabs, -1, inner)
        sent_3[pair] = both.astype(jnp.bfloat16)
        every(copies_3(pair), "start")
        share_rows = both.shape[1]
        own = pl.ds(pl.multiple_of(slab * share_rows, 16), share_rows)
        kept_3[pair] = kept_2[pair, own, :] + got_2[pair, own, :].astype(jnp.float32)

    def last_step(pair):
        every(copies_3(pair), "wait_recv")
        result = kept_3[pair]
        for k in range(slabs - 1):
            result = result + got_3[pair, k].astype(jnp.float32)
        for part in range(3):
            at = part * inner + pair * LANES
            grad_weight[:, at : at + LANES] = result[:, part * LANES : (part + 1) * LANES]

    def take_rims():
        @pl.when(has_before)
        def _():
            every(rims_up, "wait_recv")

        @pl.when(has_after)
        def _():
            every(rims_down, "wait_recv")

        @pl.when(slab == 0)
        def _():
            before[...] = jnp.zeros_like(before)
            grads_before[...] = jnp.zeros_like(grads_before)

        @pl.when(slab == slabs - 1)
        def _():
            after[...] = jnp.zeros_like(after)
            grads_after[...] = jnp.zeros_like(grads_after)

        project(before, 0, 0, REACH)
        project(after, 0, REACH + tok_rows, REACH)
        take_grads(grads_before, 0, HALF, HALF)
        take_grads(grads_after, 0, REACH + tok_rows, HALF)

    def one_pair(pair):
        seen = set()
        for tile in list(range(1, tiles - 1)) + [0, tiles - 1]:
            if tile == tiles - 2 and spread:
                pl.when(pair >= 1)(lambda: middle_step(pair - 1))
            if tile == 0:
                pl.when(pair == 0)(take_rims)
            add_to(pair, tile, attend(pair, tile), seen)
        for start in range(0, tok_rows, LANES):
            at = pl.ds(start, LANES)
            turned = rotate(key_acc[at, :], REACH + start, -1).astype(jnp.bfloat16)
            key_columns = pl.ds(pl.multiple_of(inner + pair * LANES, LANES), LANES)
            grad_proj[at, key_columns] = turned
            value_columns = pl.ds(pl.multiple_of(2 * inner + pair * LANES, LANES), LANES)
            grad_proj[at, value_columns] = value_acc[at, :].astype(jnp.bfloat16)
        if spread:
            pl.when(pair >= 2)(lambda: second_step(pair - 2))
            first_step(pair)
        else:
            for part in range(3):
                columns = pl.ds(pl.multiple_of(part * inner + pair * LANES, LANES), LANES)
                grad_weight[:, columns] = jnp.dot(
                    hidden_t[0], grad_proj[:, columns], preferred_element_type=jnp.float32
                )

    pl.loop(0, pairs)(one_pair)

    def hidden_part(start, size):
        at = pl.ds(start, size)
        grad_hidden[at, :] = lax.dot_general(
            grad_proj[at, :], w[...], (((1,), (1,)), ((), ())), preferred_element_type=jnp.float32
        ).astype(jnp.bfloat16)

    if spread:
        if pairs > 1:
            second_step(pairs - 2)
        middle_step(pairs - 1)
    hidden_part(0, step_rows)
    if spread:
        second_step(pairs - 1)
    for start in range(step_rows, tok_rows, step_rows):
        hidden_part(start, step_rows)
    pl.when(has_after)(lambda: every(rims_up, "wait_send"))
    pl.when(has_before)(lambda: every(rims_down, "wait_send"))
    if spread:
        for pair in range(pairs):
            last_step(pair)
            copy_1(pair).wait_send()
            copy_2(pair).wait_send()
            every(copies_3(pair), "wait_send")


def write_out(a, b, c, to_a, to_b, to_c, sems):
    copies = [
        pltpu.make_async_copy(source, target, sems.at[i])
        for i, (source, target) in enumerate(((a, to_a), (b, to_b), (c, to_c)))
    ]
    for copy in copies:
        copy.start()
    for copy in copies:
        copy.wait()


def local(slabs, hidden, w_qkv, doc_lengths, grad_context):
    tokens, upstream = hidden[0], grad_context[0]
    tok_rows, width = tokens.shape
    inner = upstream.shape[1]
    pairs = inner // LANES
    rows = tok_rows + 2 * REACH
    tiles = tok_rows // LANES + 1
    replicas = lax.axis_size("dp")
    share = width // (slabs * replicas)
    spread = replicas == 4 and share % 16 == 0 and slabs > 1
    near, base = angle_tables(rows, slabs, tok_rows)
    anywhere = pl.BlockSpec(memory_space=pl.ANY)
    vmem = pl.BlockSpec(memory_space=pltpu.VMEM)
    smem = pl.BlockSpec(memory_space=pltpu.SMEM)
    quarter = width // 4
    made = pltpu.VMEM if spread else jax.ShapeDtypeStruct
    summing = []
    if spread:
        summing = [
            pltpu.VMEM((2, quarter, inner), jnp.float32),
            pltpu.VMEM((pairs, 2, quarter, inner), jnp.bfloat16),
            pltpu.VMEM((pairs, 2, quarter, inner), jnp.bfloat16),
            pltpu.VMEM((pairs, quarter, inner), jnp.float32),
            pltpu.VMEM((pairs, quarter, inner), jnp.bfloat16),
            pltpu.VMEM((pairs, quarter, inner), jnp.bfloat16),
            pltpu.VMEM((pairs, share, inner), jnp.float32),
            pltpu.VMEM((pairs, slabs, share, inner), jnp.bfloat16),
            pltpu.VMEM((pairs, slabs - 1, share, inner), jnp.bfloat16),
        ] + [
            pltpu.SemaphoreType.DMA(shape)
            for shape in ((pairs,),) * 4 + ((pairs, slabs - 1),) * 2
        ]
    context, grad_hidden, grad_weight = pl.pallas_call(
        functools.partial(kernel, slabs, spread),
        out_shape=(
            made((tok_rows, inner), jnp.bfloat16),
            made((tok_rows, width), jnp.bfloat16),
            made((share if spread else width, 3 * inner), jnp.float32),
        ),
        in_specs=[smem, vmem] + [anywhere] * 4,
        out_specs=(vmem, vmem, vmem),
        scratch_shapes=[
            pltpu.VMEM((tok_rows, width), jnp.bfloat16),
            pltpu.VMEM((width, 3 * inner), jnp.bfloat16),
            pltpu.VMEM((tok_rows, inner), jnp.bfloat16),
            pltpu.VMEM((rows, 2 * LANES), jnp.float32),
            pltpu.VMEM((REACH, width), jnp.bfloat16),
            pltpu.VMEM((REACH, width), jnp.bfloat16),
            pltpu.VMEM((HALF, inner), jnp.bfloat16),
            pltpu.VMEM((HALF, inner), jnp.bfloat16),
            pltpu.VMEM((pairs, rows, LANES), jnp.bfloat16),
            pltpu.VMEM((pairs, rows, LANES), jnp.bfloat16),
            pltpu.VMEM((pairs, rows, LANES), jnp.bfloat16),
            pltpu.VMEM((pairs, LANES, rows), jnp.bfloat16),
            pltpu.VMEM((pairs, LANES, rows), jnp.bfloat16),
            pltpu.VMEM((pairs, rows, LANES), jnp.bfloat16),
            pltpu.VMEM((rows, 2 * LANES), jnp.float32),
            pltpu.VMEM((tiles, 2 * LANES, LANES), jnp.float32),
            pltpu.VMEM((tok_rows, LANES), jnp.float32),
            pltpu.VMEM((tok_rows, LANES), jnp.float32),
            pltpu.VMEM((tok_rows, 3 * inner), jnp.bfloat16),
            pltpu.VMEM(
                (2, width // 2, tok_rows) if spread else (1, width, tok_rows), jnp.bfloat16
            ),
            pltpu.SemaphoreType.DMA((4,)),
            pltpu.SemaphoreType.DMA((4,)),
            pltpu.SemaphoreType.DMA((4,)),
        ]
        + summing,
        compiler_params=pltpu.CompilerParams(
            vmem_limit_bytes=56 * 1024 * 1024, collective_id=0, has_side_effects=True
        ),
    )(
        doc_lengths, jnp.asarray(base), tokens, w_qkv, upstream, jnp.asarray(near)
    )
    if spread:
        arrays = (context, grad_hidden, grad_weight)
        context, grad_hidden, grad_weight = pl.pallas_call(
            write_out,
            out_shape=tuple(jax.ShapeDtypeStruct(a.shape, a.dtype) for a in arrays),
            in_specs=[anywhere] * 3,
            out_specs=[anywhere] * 3,
            scratch_shapes=[pltpu.SemaphoreType.DMA((3,))],
        )(*(pltpu.with_memory_space_constraint(a, pltpu.VMEM) for a in arrays))
    else:
        grad_weight = lax.psum_scatter(
            grad_weight, ("ctx", "dp"), scatter_dimension=0, tiled=True
        )
    return (context[None], grad_hidden[None], grad_weight)


def solution(mesh):
    placed = (
        P(("groups", "dp"), "ctx", None),
        P(),
        P(("groups", "dp"), None),
        P(("groups", "dp"), "ctx", None),
    )
    return jax.shard_map(
        functools.partial(local, mesh.shape["ctx"]),
        mesh=mesh,
        in_specs=placed,
        out_specs=(
            P(("groups", "dp"), "ctx", None),
            P(("groups", "dp"), "ctx", None),
            P(("groups", "ctx", "dp"), None),
        ),
        check_vma=False,
    )
```

```python
import functools

import jax
import jax.numpy as jnp
import numpy as np
from jax import lax
from jax.experimental import pallas as pl
from jax.experimental.pallas import tpu as pltpu
from jax.sharding import PartitionSpec as P

HEAD_DIM = 64
HALF = 64
LANES = 128
BLOCK = 64
HIDDEN_CUTS = 4
WINDOW = BLOCK + 2 * HALF
masked_value = -1e30
MESH = pl.DeviceIdType.MESH


def angle_tables(slabs, tok_rows):
    half_dim = HEAD_DIM // 2
    exponent = np.arange(half_dim, dtype=np.float64) * 2.0 / HEAD_DIM
    frequency = 10000.0 ** (-exponent)

    def table(positions):
        angles = positions[:, None] * frequency[None, :]
        cosine = np.tile(np.cos(angles), (1, LANES // half_dim))
        sine = np.sin(angles)
        signed = np.tile(np.concatenate([-sine, sine], axis=1), (1, LANES // HEAD_DIM))
        return np.concatenate([cosine, signed], axis=1).astype(np.float32)

    near = table(np.arange(LANES, dtype=np.float64))
    starts = np.arange(slabs * tok_rows // LANES, dtype=np.float64) * LANES
    base = table(starts).reshape(slabs, tok_rows // LANES, 1, 2 * LANES)
    return near, np.repeat(base, 8, axis=2)


def kernel(
    slabs, spread, docs_hbm, near_hbm, base_hbm, hidden_hbm, w_hbm, grads_hbm,
    context, grad_hidden, grad_weight,
    docs, near, base, hidden, w, grads, queries, kv, tables, biases, partial,
    edge_out, edge_in, grad_proj, hidden_t, load_sem, w_sem, rim_send, rim_recv, edge_send,
    edge_recv, *summing,
):
    tok_rows, width = hidden.shape
    inner = grads.shape[1]
    pairs = inner // LANES
    blocks = tok_rows // BLOCK
    doc_count = docs.shape[1]
    slab = lax.axis_index("ctx")
    offset = slab * tok_rows
    replica = lax.axis_index("dp")
    core, chip = lax.rem(replica, 2), lax.div(replica, 2)
    core_peer = {"dp": replica + 1 - 2 * core}
    chip_peer = {"dp": replica + 2 - 4 * chip}
    others = [lax.rem(slab + k, slabs) for k in range(1, slabs)]
    has_before, has_after = slab > 0, slab < slabs - 1
    barrier = pltpu.get_barrier_semaphore()

    def greet(peer):
        pl.semaphore_signal(barrier, inc=1, device_id=peer, device_id_type=MESH)

    if spread:
        for peer in [core_peer, chip_peer] + [{"ctx": other} for other in others]:
            greet(peer)
    else:
        pl.when(has_before)(lambda: greet({"ctx": slab - 1}))
        pl.when(has_after)(lambda: greet({"ctx": slab + 1}))

    def wait_for_all():
        if spread:
            pl.semaphore_wait(barrier, slabs + 1)
        else:
            pl.when(has_before)(lambda: pl.semaphore_wait(barrier, 1))
            pl.when(has_after)(lambda: pl.semaphore_wait(barrier, 1))

    def w_load(pair, part):
        return pltpu.make_async_copy(
            w_hbm.at[:, pl.ds(part * inner + pair * LANES, LANES)],
            w.at[:, pl.ds((pair * 3 + part) * LANES, LANES)],
            w_sem.at[pair, part],
        )

    def load(source, target, index):
        return pltpu.make_async_copy(source, target, load_sem.at[index])

    docs_load = load(docs_hbm, docs, 0)
    near_load = load(near_hbm, near, 1)
    base_load = load(base_hbm.at[slab], base, 2)
    grads_load = load(grads_hbm, grads, 3)
    cut = tok_rows // HIDDEN_CUTS
    hidden_loads = [
        load(hidden_hbm.at[pl.ds(i * cut, cut)], hidden.at[pl.ds(i * cut, cut)], 4 + i)
        for i in range(HIDDEN_CUTS)
    ]

    def every(copies, act):
        for copy in copies:
            getattr(copy, act)()

    every(hidden_loads, "start")
    every([w_load(0, part) for part in range(3)], "start")
    every([docs_load, near_load, base_load], "start")

    def remote(source, target, send, recv, peer):
        return pltpu.make_async_remote_copy(
            src_ref=source, dst_ref=target, send_sem=send, recv_sem=recv,
            device_id=peer, device_id_type=MESH,
        )

    def rim_up(pair):
        return remote(
            kv.at[pair, pl.ds(tok_rows, HALF)], kv.at[pair, pl.ds(0, HALF)],
            rim_send.at[pair, 0], rim_recv.at[pair, 0], {"ctx": slab + 1},
        )

    def rim_down(pair):
        return remote(
            kv.at[pair, pl.ds(HALF, HALF)], kv.at[pair, pl.ds(HALF + tok_rows, HALF)],
            rim_send.at[pair, 1], rim_recv.at[pair, 1], {"ctx": slab - 1},
        )

    def edge_up(pair):
        return remote(
            edge_out.at[pair, 1], edge_in.at[pair, 0],
            edge_send.at[pair, 1], edge_recv.at[pair, 0], {"ctx": slab + 1},
        )

    def edge_down(pair):
        return remote(
            edge_out.at[pair, 0], edge_in.at[pair, 1],
            edge_send.at[pair, 0], edge_recv.at[pair, 1], {"ctx": slab - 1},
        )

    def on_both(up, down, pair, act_up, act_down):
        pl.when(has_after)(lambda: getattr(up(pair), act_up)())
        pl.when(has_before)(lambda: getattr(down(pair), act_down)())

    lane = lax.broadcasted_iota(jnp.int32, (1, LANES), 1)
    front = lax.rem(lane, HEAD_DIM) < HEAD_DIM // 2
    low_head = lane < HEAD_DIM
    first = low_head.astype(jnp.bfloat16)
    second = (lane >= HEAD_DIM).astype(jnp.bfloat16)

    def swapped(block):
        half = HEAD_DIM // 2
        return jnp.where(
            front, pltpu.roll(block, LANES - half, 1), pltpu.roll(block, half, 1)
        )

    def rotate(block, start, sign):
        size = block.shape[0]
        turned = block * tables[pl.ds(start, size), :LANES]
        other = swapped(block) * tables[pl.ds(start, size), LANES:]
        return turned + other if sign > 0 else turned - other

    docs_load.wait()
    ends = []
    total = jnp.int32(0)
    for j in range(doc_count):
        total = total + docs[0, j]
        ends.append(total)
    key_at = lax.broadcasted_iota(jnp.int32, (WINDOW, LANES), 0)
    query_at = lax.broadcasted_iota(jnp.int32, (blocks, LANES), 0) * BLOCK + lax.rem(
        lax.broadcasted_iota(jnp.int32, (blocks, LANES), 1), BLOCK
    )
    position = query_at + offset
    opened = jnp.zeros_like(position)
    closed = jnp.full_like(position, slabs * tok_rows)
    for end in ends:
        passed = end <= position
        opened = jnp.where(passed, jnp.maximum(opened, end), opened)
        closed = jnp.where(passed, closed, jnp.minimum(closed, end))
    window_at = lax.broadcasted_iota(jnp.int32, (blocks, LANES), 0) * BLOCK - HALF + offset
    lowest = jnp.maximum(position - HALF, opened) - window_at
    highest = jnp.minimum(position + HALF, closed - 1) - window_at
    for b in range(blocks):
        seen = (key_at >= lowest[b : b + 1]) & (key_at <= highest[b : b + 1])
        biases[b] = jnp.where(seen, 0.0, masked_value).astype(jnp.float32)

    near_load.wait()
    base_load.wait()
    for i in range(tok_rows // LANES):
        at = pl.ds(i * LANES, LANES)
        base_cos, base_sin = base[i, :1, :LANES], base[i, :1, LANES:]
        tables[at, :LANES] = near[:, :LANES] * base_cos - near[:, LANES:] * base_sin
        tables[at, LANES:] = near[:, LANES:] * base_cos + near[:, :LANES] * base_sin

    @pl.when(slab == 0)
    def _():
        kv[:, :HALF, :] = jnp.zeros_like(kv[:, :HALF, :])
        edge_in[:, 0] = jnp.zeros_like(edge_in[:, 0])

    @pl.when(slab == slabs - 1)
    def _():
        kv[:, HALF + tok_rows :, :] = jnp.zeros_like(kv[:, HALF + tok_rows :, :])
        edge_in[:, 1] = jnp.zeros_like(edge_in[:, 1])

    def project(pair):
        every([w_load(pair, part) for part in range(3)], "wait")
        columns = jnp.dot(
            hidden[...],
            w[:, pair * 3 * LANES : (pair + 1) * 3 * LANES],
            preferred_element_type=jnp.float32,
        )
        own = pl.ds(HALF, tok_rows)
        queries[pair] = rotate(columns[:, :LANES], 0, 1).astype(jnp.bfloat16) * jnp.bfloat16(
            HEAD_DIM**-0.5
        )
        kv[pair, own, :LANES] = rotate(columns[:, LANES : 2 * LANES], 0, 1).astype(jnp.bfloat16)
        kv[pair, own, LANES:] = columns[:, 2 * LANES :].astype(jnp.bfloat16)

    def attend(chosen):
        last = (((1,), (1,)), ((), ()))
        nothing = jnp.zeros((2 * BLOCK, LANES), jnp.bfloat16)
        given = []
        for pair, b in chosen:
            at = pl.ds(b * BLOCK, BLOCK)
            window = kv[pair, pl.ds(b * BLOCK, WINDOW), :]
            query = queries[pair, at, :]
            grad = grads[at, pair * LANES : (pair + 1) * LANES]
            two_queries = jnp.concatenate([query * first, query * second], axis=0)
            two_grads = jnp.concatenate([grad * first, grad * second], axis=0)
            paired = jnp.concatenate(
                [
                    jnp.concatenate([two_queries, nothing], axis=1),
                    jnp.concatenate([nothing, two_grads], axis=1),
                ],
                axis=0,
            )
            both = lax.dot_general(window, paired, last, preferred_element_type=jnp.float32)
            given.append((pair, b, window, paired, both))
        chances = []
        for pair, b, window, paired, both in given:
            scores = both[:, :LANES] + biases[b]
            grad_chance = both[:, LANES:]
            raised = jnp.exp(scores - jnp.max(scores, axis=0, keepdims=True))
            inverse = 1.0 / jnp.sum(raised, axis=0, keepdims=True)
            delta = jnp.sum(raised * grad_chance, axis=0, keepdims=True) * inverse
            chance = raised * inverse
            grad_score = (chance * (grad_chance - delta)).astype(jnp.bfloat16)
            chances.append(jnp.concatenate([grad_score, chance.astype(jnp.bfloat16)], axis=1))
        pieces = {}
        for (pair, b, window, paired, _), low in zip(given, chances):
            at = pl.ds(b * BLOCK, BLOCK)
            mixed = jnp.dot(low.T, window, preferred_element_type=jnp.float32)
            query_grad = jnp.where(low_head, mixed[:BLOCK, :LANES], mixed[BLOCK:LANES, :LANES])
            mixture = jnp.where(
                low_head, mixed[LANES : LANES + BLOCK, LANES:], mixed[LANES + BLOCK :, LANES:]
            )
            context[at, pair * LANES : (pair + 1) * LANES] = mixture.astype(jnp.bfloat16)
            query_grad = rotate(query_grad * (HEAD_DIM**-0.5), b * BLOCK, -1)
            grad_proj[at, pair * 3 * LANES : (pair * 3 + 1) * LANES] = query_grad.astype(
                jnp.bfloat16
            )
            pieces[pair, b] = jnp.dot(low, paired, preferred_element_type=jnp.float32)
        return pieces

    def put(pair, block, value):
        start = (block - 1) * BLOCK
        at = pl.ds(start, BLOCK)
        turned = rotate(value[:, :LANES], start, -1).astype(jnp.bfloat16)
        grad_proj[at, (pair * 3 + 1) * LANES : (pair * 3 + 2) * LANES] = turned
        grad_proj[at, (pair * 3 + 2) * LANES : (pair * 3 + 3) * LANES] = value[:, LANES:].astype(
            jnp.bfloat16
        )

    def third(piece, k):
        return piece[k * BLOCK : (k + 1) * BLOCK]

    kept_blocks = (1, 2, blocks - 1, blocks)

    def interior(pair, group):
        sums = {}
        inside = list(range(1, blocks - 1))
        for i in range(0, len(inside), group):
            for (_, b), piece in attend([(pair, b) for b in inside[i : i + group]]).items():
                for k in range(3):
                    more = third(piece, k)
                    sums[b + k] = sums[b + k] + more if b + k in sums else more
            for block in list(sums):
                whole = block + 0 < inside[min(i + group, len(inside)) - 1] + 1 or i + group >= len(inside)
                if whole:
                    if block in (2, blocks - 1):
                        put(pair, block, sums[block] + partial[pair, kept_blocks.index(block)])
                    elif block in kept_blocks:
                        partial[pair, kept_blocks.index(block)] += sums[block]
                    else:
                        put(pair, block, sums[block])
                    del sums[block]

    def edges(*chosen):
        for pair in chosen:
            pl.when(has_before)(lambda: rim_up(pair).wait_recv())
            pl.when(has_after)(lambda: rim_down(pair).wait_recv())
        pieces = attend([(pair, b) for pair in chosen for b in (0, blocks - 1)])
        for pair in chosen:
            edge_out[pair, 0] = third(pieces[pair, 0], 0).astype(jnp.bfloat16)
            edge_out[pair, 1] = third(pieces[pair, blocks - 1], 2).astype(jnp.bfloat16)
            on_both(edge_up, edge_down, pair, "start", "start")
        for pair in chosen:
            early, late = pieces[pair, 0], pieces[pair, blocks - 1]
            partial[pair, 0] = third(early, 1)
            partial[pair, 1] = third(early, 2)
            partial[pair, 2] = third(late, 0)
            partial[pair, 3] = third(late, 1)

    def finish(pair):
        pl.when(has_before)(lambda: edge_up(pair).wait_recv())
        pl.when(has_after)(lambda: edge_down(pair).wait_recv())
        put(pair, 1, partial[pair, 0] + edge_in[pair, 0].astype(jnp.float32))
        put(pair, blocks, partial[pair, 3] + edge_in[pair, 1].astype(jnp.float32))

    def turn_hidden():
        turned_hidden = hidden[...].T
        if spread:
            share = width // (4 * slabs)
            for index in range(4 * slabs):
                z, x = index // 4, index % 4 // 2
                at = (x * slabs + z) * share
                hidden_t[index % 2, at : at + share, :] = turned_hidden[
                    index * share : (index + 1) * share
                ]
        else:
            hidden_t[0] = turned_hidden

    if spread:
        (
            kept_1, sent_1, got_1, kept_2, sent_2, got_2, kept_3, sent_3, got_3,
            sum_send, sum_recv, last_send, last_recv,
        ) = summing

        def groups_of(chunk):
            pair, is_kv = chunk
            return (pair * 3 + 1, 2) if is_kv else (pair * 3, 1)

        def transfers(chunk, step):
            start, count = groups_of(chunk)
            index = chunk[0] * 2 + chunk[1]
            at = pl.ds(start, count)
            if step < 2:
                source, target, peer = (
                    (sent_1, got_1, core_peer), (sent_2, got_2, chip_peer)
                )[step]
                return [
                    remote(
                        source.at[at], target.at[at], sum_send.at[step, index],
                        sum_recv.at[step, index], peer,
                    )
                ]
            return [
                remote(
                    sent_3.at[other, at], got_3.at[k, at], last_send.at[k, index],
                    last_recv.at[k, index], {"ctx": other},
                )
                for k, other in enumerate(others)
            ]

        def produce(chunk):
            start, count = groups_of(chunk)
            columns = slice(start * LANES, (start + count) * LANES)
            weight = grad_proj[:, columns]
            halves = [
                (jnp.dot(hidden_t[half], weight, preferred_element_type=jnp.float32), mine)
                for half, mine in ((1 - core, False), (core, True))
            ]
            for piece, mine in halves:
                for k in range(count):
                    part = piece[:, k * LANES : (k + 1) * LANES].reshape(kept_1.shape[1:])
                    if mine:
                        kept_1[start + k] = part
                    else:
                        sent_1[start + k] = part.astype(jnp.bfloat16)
                if not mine:
                    every(transfers(chunk, 0), "start")

        def forward(chunk):
            start, count = groups_of(chunk)
            at = pl.ds(start, count)
            every(transfers(chunk, 0), "wait_recv")
            sent_2[at] = (
                kept_1[at, 1 - chip] + got_1[at, 1 - chip].astype(jnp.float32)
            ).astype(jnp.bfloat16)
            every(transfers(chunk, 1), "start")
            kept_2[at] = kept_1[at, chip] + got_1[at, chip].astype(jnp.float32)

        def spread_out(chunk):
            start, count = groups_of(chunk)
            every(transfers(chunk, 1), "wait_recv")
            share = kept_3.shape[1]
            for group in range(start, start + count):
                for z in range(slabs):
                    rows = pl.ds(z * share, share)
                    both = kept_2[group, rows] + got_2[group, rows].astype(jnp.float32)
                    sent_3[z, group] = both.astype(jnp.bfloat16)
            every(transfers(chunk, 2), "start")
            own = pl.ds(pl.multiple_of(slab * share, 16), share)
            for group in range(start, start + count):
                kept_3[group] = kept_2[group, own] + got_2[group, own].astype(jnp.float32)

        def collect(chunk):
            start, count = groups_of(chunk)
            every(transfers(chunk, 2), "wait_recv")
            for group in range(start, start + count):
                pair, part = group // 3, group % 3
                column = part * inner + pair * LANES
                result = kept_3[group]
                for k in range(slabs - 1):
                    result = result + got_3[k, group].astype(jnp.float32)
                grad_weight[:, column : column + LANES] = result

    def hidden_part(start, size, cuts):
        last = (((1,), (1,)), ((), ()))
        rows = [pl.ds(start + i * (size // cuts), size // cuts) for i in range(cuts)]
        results = [
            lax.dot_general(grad_proj[at, :], w[...], last, preferred_element_type=jnp.float32)
            for at in rows
        ]
        for at, result in zip(rows, results):
            grad_hidden[at, :] = result.astype(jnp.bfloat16)

    def send_rims(pair):
        on_both(rim_up, rim_down, pair, "start", "start")

    group = 6
    every(hidden_loads, "wait")
    grads_load.start()
    for pair in range(1, pairs):
        every([w_load(pair, part) for part in range(3)], "start")
    project(0)
    wait_for_all()
    send_rims(0)
    grads_load.wait()
    if not spread or pairs != 3:
        for pair in range(1, pairs):
            project(pair)
            send_rims(pair)
        turn_hidden()
        for pair in range(pairs):
            edges(pair)
            interior(pair, group)
        for pair in range(pairs):
            finish(pair)
        for pair in range(pairs):
            for part in range(3):
                columns = slice((pair * 3 + part) * LANES, (pair * 3 + part + 1) * LANES)
                column = part * inner + pair * LANES
                grad_weight[:, column : column + LANES] = jnp.dot(
                    hidden_t[0], grad_proj[:, columns], preferred_element_type=jnp.float32
                )
        for start in range(0, tok_rows, 2 * LANES):
            hidden_part(start, 2 * LANES, 1)
    else:
        q0, q1, q2, kv0, kv1, kv2 = [(pair, is_kv) for is_kv in (0, 1) for pair in range(3)]
        plan = [
            (project, 1), (send_rims, 1), (project, 2), (send_rims, 2), (turn_hidden,),
            (edges, 0), (interior, 0, group), (produce, q0), (edges, 1, 2),
            (forward, q0), (finish, 0), (produce, kv0), (interior, 1, group), (forward, kv0),
            (produce, q1), (finish, 1), (produce, kv1), (interior, 2, group),
            (forward, q1), (spread_out, q0), (finish, 2), (produce, kv2), (forward, kv1),
            (produce, q2), (spread_out, kv0), (hidden_part, 0, tok_rows, 2), (forward, kv2),
            (forward, q2), (spread_out, q1), (spread_out, kv1), (spread_out, kv2),
            (spread_out, q2), (collect, q0), (collect, kv0), (collect, q1), (collect, kv1),
            (collect, kv2), (collect, q2),
        ]
        for act, *given in plan:
            act(*given)
        for chunk in (q0, q1, q2, kv0, kv1, kv2):
            for step in range(3):
                every(transfers(chunk, step), "wait_send")
    for pair in range(pairs):
        on_both(rim_up, rim_down, pair, "wait_send", "wait_send")
        on_both(edge_up, edge_down, pair, "wait_send", "wait_send")


def write_out(a, b, c, to_a, to_b, to_c, sems):
    copies = [
        pltpu.make_async_copy(source, target, sems.at[i])
        for i, (source, target) in enumerate(((a, to_a), (b, to_b), (c, to_c)))
    ]
    for copy in copies:
        copy.start()
    for copy in copies:
        copy.wait()


def local(slabs, hidden, w_qkv, doc_lengths, grad_context):
    tokens, upstream = hidden[0], grad_context[0]
    tok_rows, width = tokens.shape
    inner = upstream.shape[1]
    pairs = inner // LANES
    blocks = tok_rows // BLOCK
    rows = tok_rows + 2 * HALF
    replicas = lax.axis_size("dp")
    share = width // (slabs * replicas)
    spread = replicas == 4 and slabs > 1 and share % 16 == 0
    near, base = angle_tables(slabs, tok_rows)
    anywhere = pl.BlockSpec(memory_space=pl.ANY)
    vmem = pl.BlockSpec(memory_space=pltpu.VMEM)
    made = pltpu.VMEM if spread else jax.ShapeDtypeStruct
    summing = []
    if spread:
        groups = 3 * pairs
        quarter = width // 4
        for kept_shape, sent_shape, got_shape in (
            ((groups, 2, quarter),) * 3,
            ((groups, quarter),) * 3,
            ((groups, share), (slabs, groups, share), (slabs - 1, groups, share)),
        ):
            summing += [
                pltpu.VMEM((*kept_shape, LANES), jnp.float32),
                pltpu.VMEM((*sent_shape, LANES), jnp.bfloat16),
                pltpu.VMEM((*got_shape, LANES), jnp.bfloat16),
            ]
        summing += [pltpu.SemaphoreType.DMA((2, 2 * pairs))] * 2
        summing += [pltpu.SemaphoreType.DMA((slabs - 1, 2 * pairs))] * 2
    context, grad_hidden, grad_weight = pl.pallas_call(
        functools.partial(kernel, slabs, spread),
        out_shape=(
            made((tok_rows, inner), jnp.bfloat16),
            made((tok_rows, width), jnp.bfloat16),
            made((share if spread else width, 3 * inner), jnp.float32),
        ),
        in_specs=[anywhere] * 6,
        out_specs=(vmem, vmem, vmem),
        scratch_shapes=[
            pltpu.SMEM(doc_lengths.shape, jnp.int32),
            pltpu.VMEM(near.shape, jnp.float32),
            pltpu.VMEM(base.shape[1:], jnp.float32),
            pltpu.VMEM((tok_rows, width), jnp.bfloat16),
            pltpu.VMEM((width, 3 * inner), jnp.bfloat16),
            pltpu.VMEM((tok_rows, inner), jnp.bfloat16),
            pltpu.VMEM((pairs, tok_rows, LANES), jnp.bfloat16),
            pltpu.VMEM((pairs, rows, 2 * LANES), jnp.bfloat16),
            pltpu.VMEM((tok_rows, 2 * LANES), jnp.float32),
            pltpu.VMEM((blocks, WINDOW, LANES), jnp.float32),
            pltpu.VMEM((pairs, 4, BLOCK, 2 * LANES), jnp.float32),
            pltpu.VMEM((pairs, 2, BLOCK, 2 * LANES), jnp.bfloat16),
            pltpu.VMEM((pairs, 2, BLOCK, 2 * LANES), jnp.bfloat16),
            pltpu.VMEM((tok_rows, 3 * inner), jnp.bfloat16),
            pltpu.VMEM(
                (2, width // 2, tok_rows) if spread else (1, width, tok_rows), jnp.bfloat16
            ),
            pltpu.SemaphoreType.DMA((4 + HIDDEN_CUTS,)),
            pltpu.SemaphoreType.DMA((pairs, 3)),
            pltpu.SemaphoreType.DMA((pairs, 2)),
            pltpu.SemaphoreType.DMA((pairs, 2)),
            pltpu.SemaphoreType.DMA((pairs, 2)),
            pltpu.SemaphoreType.DMA((pairs, 2)),
        ]
        + summing,
        compiler_params=pltpu.CompilerParams(
            vmem_limit_bytes=54 * 1024 * 1024, collective_id=0, has_side_effects=True
        ),
    )(doc_lengths, jnp.asarray(near), jnp.asarray(base), tokens, w_qkv, upstream)
    if spread:
        arrays = (context, grad_hidden, grad_weight)
        context, grad_hidden, grad_weight = pl.pallas_call(
            write_out,
            out_shape=tuple(jax.ShapeDtypeStruct(a.shape, a.dtype) for a in arrays),
            in_specs=[anywhere] * 3,
            out_specs=[anywhere] * 3,
            scratch_shapes=[pltpu.SemaphoreType.DMA((3,))],
        )(*(pltpu.with_memory_space_constraint(a, pltpu.VMEM) for a in arrays))
    else:
        grad_weight = lax.psum_scatter(
            grad_weight, ("ctx", "dp"), scatter_dimension=0, tiled=True
        )
    return (context[None], grad_hidden[None], grad_weight)


def solution(mesh):
    placed = (
        P(("groups", "dp"), "ctx", None),
        P(),
        P(("groups", "dp"), None),
        P(("groups", "dp"), "ctx", None),
    )
    return jax.shard_map(
        functools.partial(local, mesh.shape["ctx"]),
        mesh=mesh,
        in_specs=placed,
        out_specs=(
            P(("groups", "dp"), "ctx", None),
            P(("groups", "dp"), "ctx", None),
            P(("groups", "ctx", "dp"), None),
        ),
        check_vma=False,
    )
```

```python
import functools

import jax
import jax.numpy as jnp
import numpy as np
from jax import lax
from jax.experimental import pallas as pl
from jax.experimental.pallas import tpu as pltpu
from jax.sharding import PartitionSpec as P

HEAD_DIM = 64
HALF = 64
LANES = 128
BLOCK = 64
HIDDEN_CUTS = 2
Z_FIRST = (0, 1)
WINDOW = BLOCK + 2 * HALF
masked_value = -1e30
MESH = pl.DeviceIdType.MESH


def angle_tables(slabs, tok_rows):
    half_dim = HEAD_DIM // 2
    exponent = np.arange(half_dim, dtype=np.float64) * 2.0 / HEAD_DIM
    frequency = 10000.0 ** (-exponent)

    def table(positions):
        angles = positions[:, None] * frequency[None, :]
        cosine = np.tile(np.cos(angles), (1, LANES // half_dim))
        sine = np.sin(angles)
        signed = np.tile(np.concatenate([-sine, sine], axis=1), (1, LANES // HEAD_DIM))
        return np.concatenate([cosine, signed], axis=1).astype(np.float32)

    near = table(np.arange(LANES, dtype=np.float64))
    starts = np.arange(slabs * tok_rows // LANES, dtype=np.float64) * LANES
    base = table(starts).reshape(slabs, tok_rows // LANES, 1, 2 * LANES)
    return near, np.repeat(base, 8, axis=2)


def kernel(
    slabs, spread, docs_hbm, near_hbm, base_hbm, hidden_hbm, w_hbm, grads_hbm,
    context, grad_hidden, grad_weight,
    docs, near, base, hidden, w, grads, queries, kv, tables, biases, partial,
    edge_out, edge_in, grad_proj, hidden_t, load_sem, w_sem, rim_send, rim_recv, edge_send,
    edge_recv, *summing,
):
    tok_rows, width = hidden.shape
    inner = grads.shape[1]
    pairs = inner // LANES
    blocks = tok_rows // BLOCK
    doc_count = docs.shape[1]
    slab = lax.axis_index("ctx")
    offset = slab * tok_rows
    replica = lax.axis_index("dp")
    core, chip = lax.rem(replica, 2), lax.div(replica, 2)
    core_peer = {"dp": replica + 1 - 2 * core}
    chip_peer = {"dp": replica + 2 - 4 * chip}
    others = [lax.rem(slab + k, slabs) for k in range(1, slabs)]
    has_before, has_after = slab > 0, slab < slabs - 1
    barrier = pltpu.get_barrier_semaphore()

    def greet(peer):
        pl.semaphore_signal(barrier, inc=1, device_id=peer, device_id_type=MESH)

    if spread:
        for peer in [core_peer, chip_peer] + [{"ctx": other} for other in others]:
            greet(peer)
    else:
        pl.when(has_before)(lambda: greet({"ctx": slab - 1}))
        pl.when(has_after)(lambda: greet({"ctx": slab + 1}))

    def wait_for_all():
        if spread:
            pl.semaphore_wait(barrier, slabs + 1)
        else:
            pl.when(has_before)(lambda: pl.semaphore_wait(barrier, 1))
            pl.when(has_after)(lambda: pl.semaphore_wait(barrier, 1))

    def w_load(pair, part):
        return pltpu.make_async_copy(
            w_hbm.at[:, pl.ds(part * inner + pair * LANES, LANES)],
            w.at[:, pl.ds((pair * 3 + part) * LANES, LANES)],
            w_sem.at[pair, part],
        )

    def load(source, target, index):
        return pltpu.make_async_copy(source, target, load_sem.at[index])

    docs_load = load(docs_hbm, docs, 0)
    near_load = load(near_hbm, near, 1)
    base_load = load(base_hbm.at[slab], base, 2)
    grads_load = load(grads_hbm, grads, 3)
    cut = tok_rows // HIDDEN_CUTS
    hidden_loads = [
        load(hidden_hbm.at[pl.ds(i * cut, cut)], hidden.at[pl.ds(i * cut, cut)], 4 + i)
        for i in range(HIDDEN_CUTS)
    ]

    def every(copies, act):
        for copy in copies:
            getattr(copy, act)()

    every([near_load, base_load], "start")
    every(hidden_loads, "start")
    every([w_load(0, part) for part in range(3)], "start")
    docs_load.start()

    def remote(source, target, send, recv, peer):
        return pltpu.make_async_remote_copy(
            src_ref=source, dst_ref=target, send_sem=send, recv_sem=recv,
            device_id=peer, device_id_type=MESH,
        )

    def rim_up(pair):
        return remote(
            kv.at[pair, pl.ds(tok_rows, HALF)], kv.at[pair, pl.ds(0, HALF)],
            rim_send.at[pair, 0], rim_recv.at[pair, 0], {"ctx": slab + 1},
        )

    def rim_down(pair):
        return remote(
            kv.at[pair, pl.ds(HALF, HALF)], kv.at[pair, pl.ds(HALF + tok_rows, HALF)],
            rim_send.at[pair, 1], rim_recv.at[pair, 1], {"ctx": slab - 1},
        )

    def edge_up(pair):
        return remote(
            edge_out.at[pair, 1], edge_in.at[pair, 0],
            edge_send.at[pair, 1], edge_recv.at[pair, 0], {"ctx": slab + 1},
        )

    def edge_down(pair):
        return remote(
            edge_out.at[pair, 0], edge_in.at[pair, 1],
            edge_send.at[pair, 0], edge_recv.at[pair, 1], {"ctx": slab - 1},
        )

    def on_both(up, down, pair, act_up, act_down):
        pl.when(has_after)(lambda: getattr(up(pair), act_up)())
        pl.when(has_before)(lambda: getattr(down(pair), act_down)())

    lane = lax.broadcasted_iota(jnp.int32, (1, LANES), 1)
    front = lax.rem(lane, HEAD_DIM) < HEAD_DIM // 2
    low_head = lane < HEAD_DIM
    first = low_head.astype(jnp.bfloat16)
    second = (lane >= HEAD_DIM).astype(jnp.bfloat16)

    def swapped(block):
        half = HEAD_DIM // 2
        return jnp.where(
            front, pltpu.roll(block, LANES - half, 1), pltpu.roll(block, half, 1)
        )

    def rotate(block, start, sign):
        size = block.shape[0]
        turned = block * tables[pl.ds(start, size), :LANES]
        other = swapped(block) * tables[pl.ds(start, size), LANES:]
        return turned + other if sign > 0 else turned - other

    def mask():
        docs_load.wait()
        ends = []
        total = jnp.int32(0)
        for j in range(doc_count):
            total = total + docs[0, j]
            ends.append(total)
        key_at = lax.broadcasted_iota(jnp.int32, (WINDOW, LANES), 0)
        query_at = lax.broadcasted_iota(jnp.int32, (blocks, LANES), 0) * BLOCK + lax.rem(
            lax.broadcasted_iota(jnp.int32, (blocks, LANES), 1), BLOCK
        )
        position = query_at + offset
        opened = jnp.zeros_like(position)
        closed = jnp.full_like(position, slabs * tok_rows)
        for end in ends:
            passed = end <= position
            opened = jnp.where(passed, jnp.maximum(opened, end), opened)
            closed = jnp.where(passed, closed, jnp.minimum(closed, end))
        window_at = lax.broadcasted_iota(jnp.int32, (blocks, LANES), 0) * BLOCK - HALF + offset
        lowest = jnp.maximum(position - HALF, opened) - window_at
        highest = jnp.minimum(position + HALF, closed - 1) - window_at
        for b in range(blocks):
            seen = (key_at >= lowest[b : b + 1]) & (key_at <= highest[b : b + 1])
            biases[b] = jnp.where(seen, 0.0, masked_value).astype(jnp.float32)

    near_load.wait()
    base_load.wait()
    for i in range(tok_rows // LANES):
        at = pl.ds(i * LANES, LANES)
        base_cos, base_sin = base[i, :1, :LANES], base[i, :1, LANES:]
        tables[at, :LANES] = near[:, :LANES] * base_cos - near[:, LANES:] * base_sin
        tables[at, LANES:] = near[:, LANES:] * base_cos + near[:, :LANES] * base_sin

    @pl.when(slab == 0)
    def _():
        kv[:, :HALF, :] = jnp.zeros_like(kv[:, :HALF, :])
        edge_in[:, 0] = jnp.zeros_like(edge_in[:, 0])

    @pl.when(slab == slabs - 1)
    def _():
        kv[:, HALF + tok_rows :, :] = jnp.zeros_like(kv[:, HALF + tok_rows :, :])
        edge_in[:, 1] = jnp.zeros_like(edge_in[:, 1])

    def project(pair):
        every([w_load(pair, part) for part in range(3)], "wait")
        columns = jnp.dot(
            hidden[...],
            w[:, pair * 3 * LANES : (pair + 1) * 3 * LANES],
            preferred_element_type=jnp.float32,
        )
        own = pl.ds(HALF, tok_rows)
        queries[pair] = rotate(columns[:, :LANES], 0, 1).astype(jnp.bfloat16) * jnp.bfloat16(
            HEAD_DIM**-0.5
        )
        kv[pair, own, :LANES] = rotate(columns[:, LANES : 2 * LANES], 0, 1).astype(jnp.bfloat16)
        kv[pair, own, LANES:] = columns[:, 2 * LANES :].astype(jnp.bfloat16)

    def attend(chosen):
        last = (((1,), (1,)), ((), ()))
        nothing = jnp.zeros((2 * BLOCK, LANES), jnp.bfloat16)
        given = []
        for pair, b in chosen:
            at = pl.ds(b * BLOCK, BLOCK)
            window = kv[pair, pl.ds(b * BLOCK, WINDOW), :]
            query = queries[pair, at, :]
            grad = grads[at, pair * LANES : (pair + 1) * LANES]
            two_queries = jnp.concatenate([query * first, query * second], axis=0)
            two_grads = jnp.concatenate([grad * first, grad * second], axis=0)
            paired = jnp.concatenate(
                [
                    jnp.concatenate([two_queries, nothing], axis=1),
                    jnp.concatenate([nothing, two_grads], axis=1),
                ],
                axis=0,
            )
            both = lax.dot_general(window, paired, last, preferred_element_type=jnp.float32)
            given.append((pair, b, window, paired, both))
        chances = []
        for pair, b, window, paired, both in given:
            scores = both[:, :LANES] + biases[b]
            grad_chance = both[:, LANES:]
            raised = jnp.exp(scores - jnp.max(scores, axis=0, keepdims=True))
            inverse = 1.0 / jnp.sum(raised, axis=0, keepdims=True)
            delta = jnp.sum(raised * grad_chance, axis=0, keepdims=True) * inverse
            chance = raised * inverse
            grad_score = (chance * (grad_chance - delta)).astype(jnp.bfloat16)
            chances.append(jnp.concatenate([grad_score, chance.astype(jnp.bfloat16)], axis=1))
        pieces = {}
        for (pair, b, window, paired, _), low in zip(given, chances):
            at = pl.ds(b * BLOCK, BLOCK)
            mixed = jnp.dot(low.T, window, preferred_element_type=jnp.float32)
            query_grad = jnp.where(low_head, mixed[:BLOCK, :LANES], mixed[BLOCK:LANES, :LANES])
            mixture = jnp.where(
                low_head, mixed[LANES : LANES + BLOCK, LANES:], mixed[LANES + BLOCK :, LANES:]
            )
            context[at, pair * LANES : (pair + 1) * LANES] = mixture.astype(jnp.bfloat16)
            query_grad = rotate(query_grad * (HEAD_DIM**-0.5), b * BLOCK, -1)
            grad_proj[at, pair * 3 * LANES : (pair * 3 + 1) * LANES] = query_grad.astype(
                jnp.bfloat16
            )
            pieces[pair, b] = jnp.dot(low, paired, preferred_element_type=jnp.float32)
        return pieces

    def put(pair, block, value):
        start = (block - 1) * BLOCK
        at = pl.ds(start, BLOCK)
        turned = rotate(value[:, :LANES], start, -1).astype(jnp.bfloat16)
        grad_proj[at, (pair * 3 + 1) * LANES : (pair * 3 + 2) * LANES] = turned
        grad_proj[at, (pair * 3 + 2) * LANES : (pair * 3 + 3) * LANES] = value[:, LANES:].astype(
            jnp.bfloat16
        )

    def third(piece, k):
        return piece[k * BLOCK : (k + 1) * BLOCK]

    kept_blocks = (1, 2, blocks - 1, blocks)

    started = set()

    def add_partial(pair, block, value):
        at = kept_blocks.index(block)
        if (pair, block) not in started:
            started.add((pair, block))
            partial[pair, at] = value
        elif block in (2, blocks - 1):
            put(pair, block, partial[pair, at] + value)
        else:
            partial[pair, at] += value

    def interior(pair, group):
        sums = {}
        inside = list(range(1, blocks - 1))
        for i in range(0, len(inside), group):
            for (_, b), piece in attend([(pair, b) for b in inside[i : i + group]]).items():
                for k in range(3):
                    more = third(piece, k)
                    sums[b + k] = sums[b + k] + more if b + k in sums else more
            for block in list(sums):
                whole = block + 0 < inside[min(i + group, len(inside)) - 1] + 1 or i + group >= len(inside)
                if whole:
                    if block in kept_blocks:
                        add_partial(pair, block, sums[block])
                    else:
                        put(pair, block, sums[block])
                    del sums[block]

    def edges(*chosen):
        for pair in chosen:
            pl.when(has_before)(lambda: rim_up(pair).wait_recv())
            pl.when(has_after)(lambda: rim_down(pair).wait_recv())
        pieces = attend([(pair, b) for pair in chosen for b in (0, blocks - 1)])
        for pair in chosen:
            edge_out[pair, 0] = third(pieces[pair, 0], 0).astype(jnp.bfloat16)
            edge_out[pair, 1] = third(pieces[pair, blocks - 1], 2).astype(jnp.bfloat16)
            on_both(edge_up, edge_down, pair, "start", "start")
        for pair in chosen:
            for k, block in ((1, 1), (2, 2)):
                add_partial(pair, block, third(pieces[pair, 0], k))
            for k, block in ((0, blocks - 1), (1, blocks)):
                add_partial(pair, block, third(pieces[pair, blocks - 1], k))

    def finish(pair):
        pl.when(has_before)(lambda: edge_up(pair).wait_recv())
        pl.when(has_after)(lambda: edge_down(pair).wait_recv())
        put(pair, 1, partial[pair, 0] + edge_in[pair, 0].astype(jnp.float32))
        put(pair, blocks, partial[pair, 3] + edge_in[pair, 1].astype(jnp.float32))

    def turn_hidden():
        turned_hidden = hidden[...].T
        if spread:
            share = width // (4 * slabs)
            for index in range(4 * slabs):
                z, x = index // 4, index % 4 // 2
                at = (x * slabs + z) * share
                hidden_t[index % 2, at : at + share, :] = turned_hidden[
                    index * share : (index + 1) * share
                ]
        else:
            hidden_t[0] = turned_hidden

    if spread:
        (
            kept_1, sent_1, got_1, kept_2, sent_2, got_2, kept_3, sent_3, got_3,
            kept_z, sent_z, got_z, kept_x, sent_x, got_x,
            sum_send, sum_recv, last_send, last_recv,
        ) = summing
        z_first = Z_FIRST

        def groups_of(chunk):
            pair, is_kv = chunk
            return (pair * 3 + 1, 2) if is_kv else (pair * 3, 1)

        def transfers(chunk, step):
            start, count = groups_of(chunk)
            index = chunk[0] * 2 + chunk[1]
            at = pl.ds(start, count)
            if chunk == z_first and step == 1:
                return [
                    remote(
                        sent_z.at[other], got_z.at[k], last_send.at[k, index],
                        last_recv.at[k, index], {"ctx": other},
                    )
                    for k, other in enumerate(others)
                ]
            if chunk == z_first and step == 2:
                return [
                    remote(
                        sent_x, got_x, sum_send.at[1, index], sum_recv.at[1, index], chip_peer
                    )
                ]
            if step < 2:
                source, target, peer = (
                    (sent_1, got_1, core_peer), (sent_2, got_2, chip_peer)
                )[step]
                return [
                    remote(
                        source.at[at], target.at[at], sum_send.at[step, index],
                        sum_recv.at[step, index], peer,
                    )
                ]
            return [
                remote(
                    sent_3.at[other, at], got_3.at[k, at], last_send.at[k, index],
                    last_recv.at[k, index], {"ctx": other},
                )
                for k, other in enumerate(others)
            ]

        def produce(chunk):
            start, count = groups_of(chunk)
            columns = slice(start * LANES, (start + count) * LANES)
            weight = grad_proj[:, columns]
            halves = [
                (jnp.dot(hidden_t[half], weight, preferred_element_type=jnp.float32), mine)
                for half, mine in ((1 - core, False), (core, True))
            ]
            for piece, mine in halves:
                for k in range(count):
                    part = piece[:, k * LANES : (k + 1) * LANES].reshape(kept_1.shape[1:])
                    if mine:
                        kept_1[start + k] = part
                    else:
                        sent_1[start + k] = part.astype(jnp.bfloat16)
                if not mine:
                    every(transfers(chunk, 0), "start")

        def slab_rows(z):
            share = kept_3.shape[1]
            return pl.ds(pl.multiple_of(z * share, 16), share)

        def forward(chunk):
            start, count = groups_of(chunk)
            at = pl.ds(start, count)
            every(transfers(chunk, 0), "wait_recv")
            if chunk == z_first:
                for z in range(slabs):
                    rows = slab_rows(z)
                    sent_z[z] = (
                        kept_1[at, :, rows] + got_1[at, :, rows].astype(jnp.float32)
                    ).astype(jnp.bfloat16)
                every(transfers(chunk, 1), "start")
                own = slab_rows(slab)
                kept_z[...] = kept_1[at, :, own] + got_1[at, :, own].astype(jnp.float32)
                return
            sent_2[at] = (
                kept_1[at, 1 - chip] + got_1[at, 1 - chip].astype(jnp.float32)
            ).astype(jnp.bfloat16)
            every(transfers(chunk, 1), "start")
            kept_2[at] = kept_1[at, chip] + got_1[at, chip].astype(jnp.float32)

        def spread_out(chunk):
            start, count = groups_of(chunk)
            every(transfers(chunk, 1), "wait_recv")
            if chunk == z_first:
                for side, mine in ((1 - chip, False), (chip, True)):
                    result = kept_z[:, side]
                    for k in range(slabs - 1):
                        result = result + got_z[k, :, side].astype(jnp.float32)
                    if mine:
                        kept_x[...] = result
                    else:
                        sent_x[...] = result.astype(jnp.bfloat16)
                        every(transfers(chunk, 2), "start")
                return
            share = kept_3.shape[1]
            for group in range(start, start + count):
                for z in range(slabs):
                    rows = pl.ds(z * share, share)
                    both = kept_2[group, rows] + got_2[group, rows].astype(jnp.float32)
                    sent_3[z, group] = both.astype(jnp.bfloat16)
            every(transfers(chunk, 2), "start")
            own = pl.ds(pl.multiple_of(slab * share, 16), share)
            for group in range(start, start + count):
                kept_3[group] = kept_2[group, own] + got_2[group, own].astype(jnp.float32)

        def collect(chunk):
            start, count = groups_of(chunk)
            every(transfers(chunk, 2), "wait_recv")
            for group in range(start, start + count):
                pair, part = group // 3, group % 3
                column = part * inner + pair * LANES
                if chunk == z_first:
                    result = kept_x[group - start] + got_x[group - start].astype(jnp.float32)
                else:
                    result = kept_3[group]
                    for k in range(slabs - 1):
                        result = result + got_3[k, group].astype(jnp.float32)
                grad_weight[:, column : column + LANES] = result

    def hidden_part(first_column, columns, cuts):
        last = (((1,), (1,)), ((), ()))
        size = tok_rows // cuts
        weight = w[first_column : first_column + columns, :]
        results = [
            lax.dot_general(
                grad_proj[i * size : (i + 1) * size, :], weight, last,
                preferred_element_type=jnp.float32,
            )
            for i in range(cuts)
        ]
        for i, result in enumerate(results):
            grad_hidden[
                i * size : (i + 1) * size, first_column : first_column + columns
            ] = result.astype(jnp.bfloat16)

    def send_rims(pair):
        on_both(rim_up, rim_down, pair, "start", "start")

    group = 6
    every(hidden_loads, "wait")
    grads_load.start()
    for pair in range(1, pairs):
        every([w_load(pair, part) for part in range(3)], "start")
    project(0)
    wait_for_all()
    send_rims(0)
    if not spread or pairs != 3:
        for pair in range(1, pairs):
            project(pair)
            send_rims(pair)
        turn_hidden()
        mask()
        grads_load.wait()
        for pair in range(pairs):
            edges(pair)
            interior(pair, group)
        for pair in range(pairs):
            finish(pair)
        for pair in range(pairs):
            for part in range(3):
                columns = slice((pair * 3 + part) * LANES, (pair * 3 + part + 1) * LANES)
                column = part * inner + pair * LANES
                grad_weight[:, column : column + LANES] = jnp.dot(
                    hidden_t[0], grad_proj[:, columns], preferred_element_type=jnp.float32
                )
        hidden_part(0, width, 2)
    else:
        q0, q1, q2, kv0, kv1, kv2 = [(pair, is_kv) for is_kv in (0, 1) for pair in range(3)]
        third_width = width // 3
        plan = [
            (project, 1), (send_rims, 1), (project, 2), (send_rims, 2), (turn_hidden,), (mask,),
            (grads_load.wait,), (edges, 0), (interior, 0, group), (produce, q0), (edges, 1, 2),
            (interior, 1, group), (forward, q0), (produce, q1), (finish, 0), (produce, kv0),
            (interior, 2, group), (forward, q1), (finish, 1), (produce, kv1), (forward, kv0),
            (spread_out, q0), (produce, q2), (finish, 2), (produce, kv2), (forward, kv1),
            (hidden_part, 0, third_width, 2), (forward, q2), (forward, kv2), (spread_out, q1),
            (hidden_part, third_width, 2 * third_width, 1), (spread_out, kv1), (spread_out, kv0), (spread_out, q2), (spread_out, kv2), (collect, q0), (collect, q1), (collect, kv0), (collect, kv1), (collect, q2), (collect, kv2),
        ]
        for act, *given in plan:
            act(*given)
        for chunk in (q0, q1, q2, kv0, kv1, kv2):
            for step in range(3):
                every(transfers(chunk, step), "wait_send")
    for pair in range(pairs):
        on_both(rim_up, rim_down, pair, "wait_send", "wait_send")
        on_both(edge_up, edge_down, pair, "wait_send", "wait_send")


def write_out(a, b, c, to_a, to_b, to_c, sems):
    copies = [
        pltpu.make_async_copy(source, target, sems.at[i])
        for i, (source, target) in enumerate(((a, to_a), (b, to_b), (c, to_c)))
    ]
    for copy in copies:
        copy.start()
    for copy in copies:
        copy.wait()


def local(slabs, hidden, w_qkv, doc_lengths, grad_context):
    tokens, upstream = hidden[0], grad_context[0]
    tok_rows, width = tokens.shape
    inner = upstream.shape[1]
    pairs = inner // LANES
    blocks = tok_rows // BLOCK
    rows = tok_rows + 2 * HALF
    replicas = lax.axis_size("dp")
    share = width // (slabs * replicas)
    spread = replicas == 4 and slabs > 1 and share % 16 == 0
    near, base = angle_tables(slabs, tok_rows)
    anywhere = pl.BlockSpec(memory_space=pl.ANY)
    vmem = pl.BlockSpec(memory_space=pltpu.VMEM)
    made = pltpu.VMEM if spread else jax.ShapeDtypeStruct
    summing = []
    if spread:
        groups = 3 * pairs
        quarter = width // 4
        for kept_shape, sent_shape, got_shape in (
            ((groups, 2, quarter),) * 3,
            ((groups, quarter),) * 3,
            ((groups, share), (slabs, groups, share), (slabs - 1, groups, share)),
        ):
            summing += [
                pltpu.VMEM((*kept_shape, LANES), jnp.float32),
                pltpu.VMEM((*sent_shape, LANES), jnp.bfloat16),
                pltpu.VMEM((*got_shape, LANES), jnp.bfloat16),
            ]
        count = 1 + Z_FIRST[1]
        summing += [
            pltpu.VMEM((count, 2, share, LANES), jnp.float32),
            pltpu.VMEM((slabs, count, 2, share, LANES), jnp.bfloat16),
            pltpu.VMEM((slabs - 1, count, 2, share, LANES), jnp.bfloat16),
            pltpu.VMEM((count, share, LANES), jnp.float32),
            pltpu.VMEM((count, share, LANES), jnp.bfloat16),
            pltpu.VMEM((count, share, LANES), jnp.bfloat16),
        ]
        summing += [pltpu.SemaphoreType.DMA((2, 2 * pairs))] * 2
        summing += [pltpu.SemaphoreType.DMA((slabs - 1, 2 * pairs))] * 2
    context, grad_hidden, grad_weight = pl.pallas_call(
        functools.partial(kernel, slabs, spread),
        out_shape=(
            made((tok_rows, inner), jnp.bfloat16),
            made((tok_rows, width), jnp.bfloat16),
            made((share if spread else width, 3 * inner), jnp.float32),
        ),
        in_specs=[anywhere] * 6,
        out_specs=(vmem, vmem, vmem),
        scratch_shapes=[
            pltpu.SMEM(doc_lengths.shape, jnp.int32),
            pltpu.VMEM(near.shape, jnp.float32),
            pltpu.VMEM(base.shape[1:], jnp.float32),
            pltpu.VMEM((tok_rows, width), jnp.bfloat16),
            pltpu.VMEM((width, 3 * inner), jnp.bfloat16),
            pltpu.VMEM((tok_rows, inner), jnp.bfloat16),
            pltpu.VMEM((pairs, tok_rows, LANES), jnp.bfloat16),
            pltpu.VMEM((pairs, rows, 2 * LANES), jnp.bfloat16),
            pltpu.VMEM((tok_rows, 2 * LANES), jnp.float32),
            pltpu.VMEM((blocks, WINDOW, LANES), jnp.float32),
            pltpu.VMEM((pairs, 4, BLOCK, 2 * LANES), jnp.float32),
            pltpu.VMEM((pairs, 2, BLOCK, 2 * LANES), jnp.bfloat16),
            pltpu.VMEM((pairs, 2, BLOCK, 2 * LANES), jnp.bfloat16),
            pltpu.VMEM((tok_rows, 3 * inner), jnp.bfloat16),
            pltpu.VMEM(
                (2, width // 2, tok_rows) if spread else (1, width, tok_rows), jnp.bfloat16
            ),
            pltpu.SemaphoreType.DMA((4 + HIDDEN_CUTS,)),
            pltpu.SemaphoreType.DMA((pairs, 3)),
            pltpu.SemaphoreType.DMA((pairs, 2)),
            pltpu.SemaphoreType.DMA((pairs, 2)),
            pltpu.SemaphoreType.DMA((pairs, 2)),
            pltpu.SemaphoreType.DMA((pairs, 2)),
        ]
        + summing,
        compiler_params=pltpu.CompilerParams(
            vmem_limit_bytes=54 * 1024 * 1024, collective_id=0, has_side_effects=True
        ),
    )(doc_lengths, jnp.asarray(near), jnp.asarray(base), tokens, w_qkv, upstream)
    if spread:
        arrays = (context, grad_hidden, grad_weight)
        context, grad_hidden, grad_weight = pl.pallas_call(
            write_out,
            out_shape=tuple(jax.ShapeDtypeStruct(a.shape, a.dtype) for a in arrays),
            in_specs=[anywhere] * 3,
            out_specs=[anywhere] * 3,
            scratch_shapes=[pltpu.SemaphoreType.DMA((3,))],
        )(*(pltpu.with_memory_space_constraint(a, pltpu.VMEM) for a in arrays))
    else:
        grad_weight = lax.psum_scatter(
            grad_weight, ("ctx", "dp"), scatter_dimension=0, tiled=True
        )
    return (context[None], grad_hidden[None], grad_weight)


def solution(mesh):
    placed = (
        P(("groups", "dp"), "ctx", None),
        P(),
        P(("groups", "dp"), None),
        P(("groups", "dp"), "ctx", None),
    )
    return jax.shard_map(
        functools.partial(local, mesh.shape["ctx"]),
        mesh=mesh,
        in_specs=placed,
        out_specs=(
            P(("groups", "dp"), "ctx", None),
            P(("groups", "dp"), "ctx", None),
            P(("groups", "ctx", "dp"), None),
        ),
        check_vma=False,
    )
```

```python
import functools

import jax
import jax.numpy as jnp
import numpy as np
from jax import lax
from jax.experimental import pallas as pl
from jax.experimental.pallas import tpu as pltpu
from jax.sharding import PartitionSpec as P

HEAD_DIM = 64
HALF = 64
LANES = 128
BLOCK = 64
HIDDEN_CUTS = 2
Z_FIRST = (0, 1)
WINDOW = BLOCK + 2 * HALF
masked_value = -1e30
MESH = pl.DeviceIdType.MESH


def angle_tables(slabs, tok_rows):
    half_dim = HEAD_DIM // 2
    exponent = np.arange(half_dim, dtype=np.float64) * 2.0 / HEAD_DIM
    frequency = 10000.0 ** (-exponent)

    def table(positions):
        angles = positions[:, None] * frequency[None, :]
        cosine = np.tile(np.cos(angles), (1, LANES // half_dim))
        sine = np.sin(angles)
        signed = np.tile(np.concatenate([-sine, sine], axis=1), (1, LANES // HEAD_DIM))
        return np.concatenate([cosine, signed], axis=1).astype(np.float32)

    near = table(np.arange(LANES, dtype=np.float64))
    starts = np.arange(slabs * tok_rows // LANES, dtype=np.float64) * LANES
    base = table(starts).reshape(slabs, tok_rows // LANES, 1, 2 * LANES)
    return near, np.repeat(base, 8, axis=2)


def kernel(
    slabs, spread, docs_hbm, near_hbm, base_hbm, hidden_hbm, w_hbm, grads_hbm,
    context, grad_hidden, grad_weight,
    docs, near, base, hidden, w, grads, queries, kv, tables, biases, partial,
    edge_out, edge_in, grad_proj, hidden_t, load_sem, w_sem, rim_send, rim_recv, edge_send,
    edge_recv, *summing,
):
    tok_rows, width = hidden.shape
    inner = grads.shape[1]
    pairs = inner // LANES
    blocks = tok_rows // BLOCK
    doc_count = docs.shape[1]
    slab = lax.axis_index("ctx")
    offset = slab * tok_rows
    replica = lax.axis_index("dp")
    core, chip = lax.rem(replica, 2), lax.div(replica, 2)
    core_peer = {"dp": replica + 1 - 2 * core}
    chip_peer = {"dp": replica + 2 - 4 * chip}
    others = [lax.rem(slab + k, slabs) for k in range(1, slabs)]
    has_before, has_after = slab > 0, slab < slabs - 1
    barrier = pltpu.get_barrier_semaphore()

    def greet(peer):
        pl.semaphore_signal(barrier, inc=1, device_id=peer, device_id_type=MESH)

    if spread:
        for peer in [core_peer, chip_peer] + [{"ctx": other} for other in others]:
            greet(peer)
    else:
        pl.when(has_before)(lambda: greet({"ctx": slab - 1}))
        pl.when(has_after)(lambda: greet({"ctx": slab + 1}))

    def wait_for_all():
        if spread:
            pl.semaphore_wait(barrier, slabs + 1)
        else:
            pl.when(has_before)(lambda: pl.semaphore_wait(barrier, 1))
            pl.when(has_after)(lambda: pl.semaphore_wait(barrier, 1))

    def w_load(pair, part):
        return pltpu.make_async_copy(
            w_hbm.at[:, pl.ds(part * inner + pair * LANES, LANES)],
            w.at[:, pl.ds((pair * 3 + part) * LANES, LANES)],
            w_sem.at[pair, part],
        )

    def load(source, target, index):
        return pltpu.make_async_copy(source, target, load_sem.at[index])

    docs_load = load(docs_hbm, docs, 0)
    near_load = load(near_hbm, near, 1)
    base_load = load(base_hbm.at[slab], base, 2)
    grads_load = load(grads_hbm, grads, 3)
    cut = tok_rows // HIDDEN_CUTS
    hidden_loads = [
        load(hidden_hbm.at[pl.ds(i * cut, cut)], hidden.at[pl.ds(i * cut, cut)], 4 + i)
        for i in range(HIDDEN_CUTS)
    ]

    def every(copies, act):
        for copy in copies:
            getattr(copy, act)()

    every([near_load, base_load], "start")
    every(hidden_loads, "start")
    every([w_load(0, part) for part in range(3)], "start")
    docs_load.start()

    def remote(source, target, send, recv, peer):
        return pltpu.make_async_remote_copy(
            src_ref=source, dst_ref=target, send_sem=send, recv_sem=recv,
            device_id=peer, device_id_type=MESH,
        )

    def rim_up(pair):
        return remote(
            kv.at[pair, pl.ds(tok_rows, HALF)], kv.at[pair, pl.ds(0, HALF)],
            rim_send.at[pair, 0], rim_recv.at[pair, 0], {"ctx": slab + 1},
        )

    def rim_down(pair):
        return remote(
            kv.at[pair, pl.ds(HALF, HALF)], kv.at[pair, pl.ds(HALF + tok_rows, HALF)],
            rim_send.at[pair, 1], rim_recv.at[pair, 1], {"ctx": slab - 1},
        )

    def edge_up(pair):
        return remote(
            edge_out.at[pair, 1], edge_in.at[pair, 0],
            edge_send.at[pair, 1], edge_recv.at[pair, 0], {"ctx": slab + 1},
        )

    def edge_down(pair):
        return remote(
            edge_out.at[pair, 0], edge_in.at[pair, 1],
            edge_send.at[pair, 0], edge_recv.at[pair, 1], {"ctx": slab - 1},
        )

    def on_both(up, down, pair, act_up, act_down):
        pl.when(has_after)(lambda: getattr(up(pair), act_up)())
        pl.when(has_before)(lambda: getattr(down(pair), act_down)())

    lane = lax.broadcasted_iota(jnp.int32, (1, LANES), 1)
    front = lax.rem(lane, HEAD_DIM) < HEAD_DIM // 2
    low_head = lane < HEAD_DIM
    first = low_head.astype(jnp.bfloat16)
    second = (lane >= HEAD_DIM).astype(jnp.bfloat16)

    def swapped(block):
        half = HEAD_DIM // 2
        return jnp.where(
            front, pltpu.roll(block, LANES - half, 1), pltpu.roll(block, half, 1)
        )

    def rotate(block, start, sign):
        size = block.shape[0]
        turned = block * tables[pl.ds(start, size), :LANES]
        other = swapped(block) * tables[pl.ds(start, size), LANES:]
        return turned + other if sign > 0 else turned - other

    def mask():
        docs_load.wait()
        ends = []
        total = jnp.int32(0)
        for j in range(doc_count):
            total = total + docs[0, j]
            ends.append(total)
        key_at = lax.broadcasted_iota(jnp.int32, (WINDOW, LANES), 0)
        query_at = lax.broadcasted_iota(jnp.int32, (blocks, LANES), 0) * BLOCK + lax.rem(
            lax.broadcasted_iota(jnp.int32, (blocks, LANES), 1), BLOCK
        )
        position = query_at + offset
        opened = jnp.zeros_like(position)
        closed = jnp.full_like(position, slabs * tok_rows)
        for end in ends:
            passed = end <= position
            opened = jnp.where(passed, jnp.maximum(opened, end), opened)
            closed = jnp.where(passed, closed, jnp.minimum(closed, end))
        window_at = lax.broadcasted_iota(jnp.int32, (blocks, LANES), 0) * BLOCK - HALF + offset
        lowest = jnp.maximum(position - HALF, opened) - window_at
        highest = jnp.minimum(position + HALF, closed - 1) - window_at
        for b in range(blocks):
            seen = (key_at >= lowest[b : b + 1]) & (key_at <= highest[b : b + 1])
            biases[b] = jnp.where(seen, 0.0, masked_value).astype(jnp.float32)

    near_load.wait()
    base_load.wait()
    for i in range(tok_rows // LANES):
        at = pl.ds(i * LANES, LANES)
        base_cos, base_sin = base[i, :1, :LANES], base[i, :1, LANES:]
        tables[at, :LANES] = near[:, :LANES] * base_cos - near[:, LANES:] * base_sin
        tables[at, LANES:] = near[:, LANES:] * base_cos + near[:, :LANES] * base_sin

    @pl.when(slab == 0)
    def _():
        kv[:, :HALF, :] = jnp.zeros_like(kv[:, :HALF, :])
        edge_in[:, 0] = jnp.zeros_like(edge_in[:, 0])

    @pl.when(slab == slabs - 1)
    def _():
        kv[:, HALF + tok_rows :, :] = jnp.zeros_like(kv[:, HALF + tok_rows :, :])
        edge_in[:, 1] = jnp.zeros_like(edge_in[:, 1])

    def project(pair, ahead=False):
        if not ahead:
            every([w_load(pair, part) for part in range(3)], "wait")
        columns = jnp.dot(
            hidden[...],
            w[:, pair * 3 * LANES : (pair + 1) * 3 * LANES],
            preferred_element_type=jnp.float32,
        )
        queries[pair] = rotate(columns[:, :LANES], 0, 1).astype(jnp.bfloat16) * jnp.bfloat16(
            HEAD_DIM**-0.5
        )
        inside = slice(HALF, tok_rows - HALF) if ahead else slice(0, tok_rows)
        size = inside.stop - inside.start
        own = pl.ds(HALF + inside.start, size)
        kv[pair, own, :LANES] = rotate(
            columns[inside, LANES : 2 * LANES], inside.start, 1
        ).astype(jnp.bfloat16)
        kv[pair, own, LANES:] = columns[inside, 2 * LANES :].astype(jnp.bfloat16)

    def project_rims(pair):
        every([w_load(pair, part) for part in range(3)], "wait")
        starts = (0, tok_rows - HALF)
        columns = jnp.dot(
            jnp.concatenate([hidden[start : start + HALF, :] for start in starts], axis=0),
            w[:, (pair * 3 + 1) * LANES : (pair + 1) * 3 * LANES],
            preferred_element_type=jnp.float32,
        )
        for i, start in enumerate(starts):
            own = pl.ds(HALF + start, HALF)
            piece = columns[i * HALF : (i + 1) * HALF]
            kv[pair, own, :LANES] = rotate(piece[:, :LANES], start, 1).astype(jnp.bfloat16)
            kv[pair, own, LANES:] = piece[:, LANES:].astype(jnp.bfloat16)

    def attend(chosen):
        last = (((1,), (1,)), ((), ()))
        nothing = jnp.zeros((2 * BLOCK, LANES), jnp.bfloat16)
        given = []
        for pair, b in chosen:
            at = pl.ds(b * BLOCK, BLOCK)
            window = kv[pair, pl.ds(b * BLOCK, WINDOW), :]
            query = queries[pair, at, :]
            grad = grads[at, pair * LANES : (pair + 1) * LANES]
            two_queries = jnp.concatenate([query * first, query * second], axis=0)
            two_grads = jnp.concatenate([grad * first, grad * second], axis=0)
            paired = jnp.concatenate(
                [
                    jnp.concatenate([two_queries, nothing], axis=1),
                    jnp.concatenate([nothing, two_grads], axis=1),
                ],
                axis=0,
            )
            both = lax.dot_general(window, paired, last, preferred_element_type=jnp.float32)
            given.append((pair, b, window, paired, both))
        chances = []
        for pair, b, window, paired, both in given:
            scores = both[:, :LANES] + biases[b]
            grad_chance = both[:, LANES:]
            raised = jnp.exp(scores - jnp.max(scores, axis=0, keepdims=True))
            inverse = 1.0 / jnp.sum(raised, axis=0, keepdims=True)
            delta = jnp.sum(raised * grad_chance, axis=0, keepdims=True) * inverse
            chance = raised * inverse
            grad_score = (chance * (grad_chance - delta)).astype(jnp.bfloat16)
            chances.append(jnp.concatenate([grad_score, chance.astype(jnp.bfloat16)], axis=1))
        pieces = {}
        for (pair, b, window, paired, _), low in zip(given, chances):
            at = pl.ds(b * BLOCK, BLOCK)
            mixed = jnp.dot(low.T, window, preferred_element_type=jnp.float32)
            query_grad = jnp.where(low_head, mixed[:BLOCK, :LANES], mixed[BLOCK:LANES, :LANES])
            mixture = jnp.where(
                low_head, mixed[LANES : LANES + BLOCK, LANES:], mixed[LANES + BLOCK :, LANES:]
            )
            context[at, pair * LANES : (pair + 1) * LANES] = mixture.astype(jnp.bfloat16)
            query_grad = rotate(query_grad * (HEAD_DIM**-0.5), b * BLOCK, -1)
            grad_proj[at, pair * 3 * LANES : (pair * 3 + 1) * LANES] = query_grad.astype(
                jnp.bfloat16
            )
            pieces[pair, b] = jnp.dot(low, paired, preferred_element_type=jnp.float32)
        return pieces

    def put(pair, block, value):
        start = (block - 1) * BLOCK
        at = pl.ds(start, BLOCK)
        turned = rotate(value[:, :LANES], start, -1).astype(jnp.bfloat16)
        grad_proj[at, (pair * 3 + 1) * LANES : (pair * 3 + 2) * LANES] = turned
        grad_proj[at, (pair * 3 + 2) * LANES : (pair * 3 + 3) * LANES] = value[:, LANES:].astype(
            jnp.bfloat16
        )

    def third(piece, k):
        return piece[k * BLOCK : (k + 1) * BLOCK]

    kept_blocks = (1, 2, blocks - 1, blocks)

    started = set()

    def add_partial(pair, block, value):
        at = kept_blocks.index(block)
        if (pair, block) not in started:
            started.add((pair, block))
            partial[pair, at] = value
        elif block in (2, blocks - 1):
            put(pair, block, partial[pair, at] + value)
        else:
            partial[pair, at] += value

    def interior(pair, group):
        sums = {}
        inside = list(range(1, blocks - 1))
        for i in range(0, len(inside), group):
            for (_, b), piece in attend([(pair, b) for b in inside[i : i + group]]).items():
                for k in range(3):
                    more = third(piece, k)
                    sums[b + k] = sums[b + k] + more if b + k in sums else more
            for block in list(sums):
                whole = block + 0 < inside[min(i + group, len(inside)) - 1] + 1 or i + group >= len(inside)
                if whole:
                    if block in kept_blocks:
                        add_partial(pair, block, sums[block])
                    else:
                        put(pair, block, sums[block])
                    del sums[block]

    def edges(*chosen):
        for pair in chosen:
            pl.when(has_before)(lambda: rim_up(pair).wait_recv())
            pl.when(has_after)(lambda: rim_down(pair).wait_recv())
        pieces = attend([(pair, b) for pair in chosen for b in (0, blocks - 1)])
        for pair in chosen:
            edge_out[pair, 0] = third(pieces[pair, 0], 0).astype(jnp.bfloat16)
            edge_out[pair, 1] = third(pieces[pair, blocks - 1], 2).astype(jnp.bfloat16)
            on_both(edge_up, edge_down, pair, "start", "start")
        for pair in chosen:
            for k, block in ((1, 1), (2, 2)):
                add_partial(pair, block, third(pieces[pair, 0], k))
            for k, block in ((0, blocks - 1), (1, blocks)):
                add_partial(pair, block, third(pieces[pair, blocks - 1], k))

    def finish(pair):
        pl.when(has_before)(lambda: edge_up(pair).wait_recv())
        pl.when(has_after)(lambda: edge_down(pair).wait_recv())
        put(pair, 1, partial[pair, 0] + edge_in[pair, 0].astype(jnp.float32))
        put(pair, blocks, partial[pair, 3] + edge_in[pair, 1].astype(jnp.float32))

    def turn_hidden():
        turned_hidden = hidden[...].T
        if spread:
            share = width // (4 * slabs)
            for index in range(4 * slabs):
                z, x = index // 4, index % 4 // 2
                at = (x * slabs + z) * share
                hidden_t[index % 2, at : at + share, :] = turned_hidden[
                    index * share : (index + 1) * share
                ]
        else:
            hidden_t[0] = turned_hidden

    if spread:
        (
            kept_1, sent_1, got_1, kept_2, sent_2, got_2, kept_3, sent_3, got_3,
            kept_z, sent_z, got_z, kept_x, sent_x, got_x,
            sum_send, sum_recv, last_send, last_recv,
        ) = summing
        z_first = Z_FIRST

        def groups_of(chunk):
            pair, is_kv = chunk
            return (pair * 3 + 1, 2) if is_kv else (pair * 3, 1)

        def transfers(chunk, step):
            start, count = groups_of(chunk)
            index = chunk[0] * 2 + chunk[1]
            at = pl.ds(start, count)
            if chunk == z_first and step == 1:
                return [
                    remote(
                        sent_z.at[other], got_z.at[k], last_send.at[k, index],
                        last_recv.at[k, index], {"ctx": other},
                    )
                    for k, other in enumerate(others)
                ]
            if chunk == z_first and step == 2:
                return [
                    remote(
                        sent_x, got_x, sum_send.at[1, index], sum_recv.at[1, index], chip_peer
                    )
                ]
            if step < 2:
                source, target, peer = (
                    (sent_1, got_1, core_peer), (sent_2, got_2, chip_peer)
                )[step]
                return [
                    remote(
                        source.at[at], target.at[at], sum_send.at[step, index],
                        sum_recv.at[step, index], peer,
                    )
                ]
            return [
                remote(
                    sent_3.at[other, at], got_3.at[k, at], last_send.at[k, index],
                    last_recv.at[k, index], {"ctx": other},
                )
                for k, other in enumerate(others)
            ]

        def produce(chunk):
            start, count = groups_of(chunk)
            columns = slice(start * LANES, (start + count) * LANES)
            weight = grad_proj[:, columns]
            halves = [
                (jnp.dot(hidden_t[half], weight, preferred_element_type=jnp.float32), mine)
                for half, mine in ((1 - core, False), (core, True))
            ]
            for piece, mine in halves:
                for k in range(count):
                    part = piece[:, k * LANES : (k + 1) * LANES].reshape(kept_1.shape[1:])
                    if mine:
                        kept_1[start + k] = part
                    else:
                        sent_1[start + k] = part.astype(jnp.bfloat16)
                if not mine:
                    every(transfers(chunk, 0), "start")

        def slab_rows(z):
            share = kept_3.shape[1]
            return pl.ds(pl.multiple_of(z * share, 16), share)

        def forward(chunk):
            start, count = groups_of(chunk)
            at = pl.ds(start, count)
            every(transfers(chunk, 0), "wait_recv")
            if chunk == z_first:
                for z in range(slabs):
                    rows = slab_rows(z)
                    sent_z[z] = (
                        kept_1[at, :, rows] + got_1[at, :, rows].astype(jnp.float32)
                    ).astype(jnp.bfloat16)
                every(transfers(chunk, 1), "start")
                own = slab_rows(slab)
                kept_z[...] = kept_1[at, :, own] + got_1[at, :, own].astype(jnp.float32)
                return
            sent_2[at] = (
                kept_1[at, 1 - chip] + got_1[at, 1 - chip].astype(jnp.float32)
            ).astype(jnp.bfloat16)
            every(transfers(chunk, 1), "start")
            kept_2[at] = kept_1[at, chip] + got_1[at, chip].astype(jnp.float32)

        def spread_out(chunk):
            start, count = groups_of(chunk)
            every(transfers(chunk, 1), "wait_recv")
            if chunk == z_first:
                for side, mine in ((1 - chip, False), (chip, True)):
                    result = kept_z[:, side]
                    for k in range(slabs - 1):
                        result = result + got_z[k, :, side].astype(jnp.float32)
                    if mine:
                        kept_x[...] = result
                    else:
                        sent_x[...] = result.astype(jnp.bfloat16)
                        every(transfers(chunk, 2), "start")
                return
            share = kept_3.shape[1]
            for group in range(start, start + count):
                for z in range(slabs):
                    rows = pl.ds(z * share, share)
                    both = kept_2[group, rows] + got_2[group, rows].astype(jnp.float32)
                    sent_3[z, group] = both.astype(jnp.bfloat16)
            every(transfers(chunk, 2), "start")
            own = pl.ds(pl.multiple_of(slab * share, 16), share)
            for group in range(start, start + count):
                kept_3[group] = kept_2[group, own] + got_2[group, own].astype(jnp.float32)

        def collect(chunk):
            start, count = groups_of(chunk)
            every(transfers(chunk, 2), "wait_recv")
            for group in range(start, start + count):
                pair, part = group // 3, group % 3
                column = part * inner + pair * LANES
                if chunk == z_first:
                    result = kept_x[group - start] + got_x[group - start].astype(jnp.float32)
                else:
                    result = kept_3[group]
                    for k in range(slabs - 1):
                        result = result + got_3[k, group].astype(jnp.float32)
                grad_weight[:, column : column + LANES] = result

    def hidden_part(first_column, columns, cuts):
        last = (((1,), (1,)), ((), ()))
        size = tok_rows // cuts
        weight = w[first_column : first_column + columns, :]
        results = [
            lax.dot_general(
                grad_proj[i * size : (i + 1) * size, :], weight, last,
                preferred_element_type=jnp.float32,
            )
            for i in range(cuts)
        ]
        for i, result in enumerate(results):
            grad_hidden[
                i * size : (i + 1) * size, first_column : first_column + columns
            ] = result.astype(jnp.bfloat16)

    def send_rims(pair):
        on_both(rim_up, rim_down, pair, "start", "start")

    group = 6
    every(hidden_loads, "wait")
    grads_load.start()
    for pair in range(1, pairs):
        every([w_load(pair, part) for part in range(3)], "start")
    project_rims(0)
    wait_for_all()
    send_rims(0)
    project(0, True)
    if not spread or pairs != 3:
        for pair in range(1, pairs):
            project(pair)
            send_rims(pair)
        turn_hidden()
        mask()
        grads_load.wait()
        for pair in range(pairs):
            edges(pair)
            interior(pair, group)
        for pair in range(pairs):
            finish(pair)
        for pair in range(pairs):
            for part in range(3):
                columns = slice((pair * 3 + part) * LANES, (pair * 3 + part + 1) * LANES)
                column = part * inner + pair * LANES
                grad_weight[:, column : column + LANES] = jnp.dot(
                    hidden_t[0], grad_proj[:, columns], preferred_element_type=jnp.float32
                )
        hidden_part(0, width, 2)
    else:
        q0, q1, q2, kv0, kv1, kv2 = [(pair, is_kv) for is_kv in (0, 1) for pair in range(3)]
        third_width = width // 3
        plan = [
            (project, 1), (send_rims, 1), (project, 2), (send_rims, 2), (turn_hidden,), (mask,),
            (grads_load.wait,), (edges, 0), (interior, 0, group), (produce, q0), (edges, 1, 2),
            (interior, 1, group), (forward, q0), (produce, q1), (finish, 0), (produce, kv0),
            (interior, 2, group), (forward, q1), (forward, kv0), (finish, 1), (produce, kv1),
            (spread_out, q0), (produce, q2), (finish, 2), (produce, kv2), (forward, kv1),
            (hidden_part, 0, third_width, 2), (forward, q2), (forward, kv2), (spread_out, q1),
            (hidden_part, third_width, 2 * third_width, 1), (spread_out, kv1), (spread_out, kv0), (spread_out, q2), (spread_out, kv2), (collect, q0), (collect, q1), (collect, kv0), (collect, kv1), (collect, q2), (collect, kv2),
        ]
        for act, *given in plan:
            act(*given)
        for chunk in (q0, q1, q2, kv0, kv1, kv2):
            for step in range(3):
                every(transfers(chunk, step), "wait_send")
    for pair in range(pairs):
        on_both(rim_up, rim_down, pair, "wait_send", "wait_send")
        on_both(edge_up, edge_down, pair, "wait_send", "wait_send")


def write_out(a, b, c, to_a, to_b, to_c, sems):
    copies = [
        pltpu.make_async_copy(source, target, sems.at[i])
        for i, (source, target) in enumerate(((a, to_a), (b, to_b), (c, to_c)))
    ]
    for copy in copies:
        copy.start()
    for copy in copies:
        copy.wait()


def local(slabs, hidden, w_qkv, doc_lengths, grad_context):
    tokens, upstream = hidden[0], grad_context[0]
    tok_rows, width = tokens.shape
    inner = upstream.shape[1]
    pairs = inner // LANES
    blocks = tok_rows // BLOCK
    rows = tok_rows + 2 * HALF
    replicas = lax.axis_size("dp")
    share = width // (slabs * replicas)
    spread = replicas == 4 and slabs > 1 and share % 16 == 0
    near, base = angle_tables(slabs, tok_rows)
    anywhere = pl.BlockSpec(memory_space=pl.ANY)
    vmem = pl.BlockSpec(memory_space=pltpu.VMEM)
    made = pltpu.VMEM if spread else jax.ShapeDtypeStruct
    summing = []
    if spread:
        groups = 3 * pairs
        quarter = width // 4
        for kept_shape, sent_shape, got_shape in (
            ((groups, 2, quarter),) * 3,
            ((groups, quarter),) * 3,
            ((groups, share), (slabs, groups, share), (slabs - 1, groups, share)),
        ):
            summing += [
                pltpu.VMEM((*kept_shape, LANES), jnp.float32),
                pltpu.VMEM((*sent_shape, LANES), jnp.bfloat16),
                pltpu.VMEM((*got_shape, LANES), jnp.bfloat16),
            ]
        count = 1 + Z_FIRST[1]
        summing += [
            pltpu.VMEM((count, 2, share, LANES), jnp.float32),
            pltpu.VMEM((slabs, count, 2, share, LANES), jnp.bfloat16),
            pltpu.VMEM((slabs - 1, count, 2, share, LANES), jnp.bfloat16),
            pltpu.VMEM((count, share, LANES), jnp.float32),
            pltpu.VMEM((count, share, LANES), jnp.bfloat16),
            pltpu.VMEM((count, share, LANES), jnp.bfloat16),
        ]
        summing += [pltpu.SemaphoreType.DMA((2, 2 * pairs))] * 2
        summing += [pltpu.SemaphoreType.DMA((slabs - 1, 2 * pairs))] * 2
    context, grad_hidden, grad_weight = pl.pallas_call(
        functools.partial(kernel, slabs, spread),
        out_shape=(
            made((tok_rows, inner), jnp.bfloat16),
            made((tok_rows, width), jnp.bfloat16),
            made((share if spread else width, 3 * inner), jnp.float32),
        ),
        in_specs=[anywhere] * 6,
        out_specs=(vmem, vmem, vmem),
        scratch_shapes=[
            pltpu.SMEM(doc_lengths.shape, jnp.int32),
            pltpu.VMEM(near.shape, jnp.float32),
            pltpu.VMEM(base.shape[1:], jnp.float32),
            pltpu.VMEM((tok_rows, width), jnp.bfloat16),
            pltpu.VMEM((width, 3 * inner), jnp.bfloat16),
            pltpu.VMEM((tok_rows, inner), jnp.bfloat16),
            pltpu.VMEM((pairs, tok_rows, LANES), jnp.bfloat16),
            pltpu.VMEM((pairs, rows, 2 * LANES), jnp.bfloat16),
            pltpu.VMEM((tok_rows, 2 * LANES), jnp.float32),
            pltpu.VMEM((blocks, WINDOW, LANES), jnp.float32),
            pltpu.VMEM((pairs, 4, BLOCK, 2 * LANES), jnp.float32),
            pltpu.VMEM((pairs, 2, BLOCK, 2 * LANES), jnp.bfloat16),
            pltpu.VMEM((pairs, 2, BLOCK, 2 * LANES), jnp.bfloat16),
            pltpu.VMEM((tok_rows, 3 * inner), jnp.bfloat16),
            pltpu.VMEM(
                (2, width // 2, tok_rows) if spread else (1, width, tok_rows), jnp.bfloat16
            ),
            pltpu.SemaphoreType.DMA((4 + HIDDEN_CUTS,)),
            pltpu.SemaphoreType.DMA((pairs, 3)),
            pltpu.SemaphoreType.DMA((pairs, 2)),
            pltpu.SemaphoreType.DMA((pairs, 2)),
            pltpu.SemaphoreType.DMA((pairs, 2)),
            pltpu.SemaphoreType.DMA((pairs, 2)),
        ]
        + summing,
        compiler_params=pltpu.CompilerParams(
            vmem_limit_bytes=54 * 1024 * 1024, collective_id=0, has_side_effects=True
        ),
    )(doc_lengths, jnp.asarray(near), jnp.asarray(base), tokens, w_qkv, upstream)
    if spread:
        arrays = (context, grad_hidden, grad_weight)
        context, grad_hidden, grad_weight = pl.pallas_call(
            write_out,
            out_shape=tuple(jax.ShapeDtypeStruct(a.shape, a.dtype) for a in arrays),
            in_specs=[anywhere] * 3,
            out_specs=[anywhere] * 3,
            scratch_shapes=[pltpu.SemaphoreType.DMA((3,))],
        )(*(pltpu.with_memory_space_constraint(a, pltpu.VMEM) for a in arrays))
    else:
        grad_weight = lax.psum_scatter(
            grad_weight, ("ctx", "dp"), scatter_dimension=0, tiled=True
        )
    return (context[None], grad_hidden[None], grad_weight)


def solution(mesh):
    placed = (
        P(("groups", "dp"), "ctx", None),
        P(),
        P(("groups", "dp"), None),
        P(("groups", "dp"), "ctx", None),
    )
    return jax.shard_map(
        functools.partial(local, mesh.shape["ctx"]),
        mesh=mesh,
        in_specs=placed,
        out_specs=(
            P(("groups", "dp"), "ctx", None),
            P(("groups", "dp"), "ctx", None),
            P(("groups", "ctx", "dp"), None),
        ),
        check_vma=False,
    )
```
